512 devices in a mesh: dp: 32 (over z, x_hi), replica: 16 (over y, x_lo, core).
Axes of the slice: x: 4 (x_hi: 2, x_lo: 2; x = x_hi * 2 + x_lo), y: 4, z: 16, core: 2. Of those that a mesh axis runs over, the one named last changes fastest.
Arguments:
- grad_parts: bfloat16 [1024, 256, 512], P('dp', 'replica'), may hold values from -1.1953125 to 1.1953125
- master_weight: float32 [8192, 512], P(('dp', 'replica')), may hold values from -0.0625 to 0.0625
- moment_one: float32 [8192, 512], P(('dp', 'replica')), may hold values from -1.8 to 1.8
- moment_two: float32 [8192, 512], P(('dp', 'replica')), may hold values from 0.05 to 2
- queries: bfloat16 [16, 4096, 4096], P('replica', 'dp'), may hold values from -5 to 5
- keys_in: bfloat16 [16, 4096, 512], P('replica', 'dp'), may hold values from -5 to 5
- hidden: bfloat16 [16, 4096, 8192], P('replica', 'dp'), may hold values from -6 to 6
- segment_ids: int32 [16, 4096], P('replica', 'dp'), may hold values from 0 to 20, never falling along the last dimension, each value on 1 to 384 neighbouring positions
- packed_len: int32 [16], P('replica'), may hold values from 2048 to 4096
Outputs:
- new_master: float32 [8192, 512], P(('dp', 'replica'))
- new_first: float32 [8192, 512], P(('dp', 'replica'))
- new_second: float32 [8192, 512], P(('dp', 'replica'))
- attended: bfloat16 [16, 4096, 4096], P('replica', 'dp')
The draws below stay inside these ranges and needn't reach their ends.
Inputs may be any that keep to these rules, and one draw needn't show every extreme that they name: `segment_ids`: on each replica the numbers never fall along positions, and each prompt covers at most 384 positions, one exactly that many.
All inputs are finite; a program needn't handle non-finite values.
Results may differ from the reference program's by a relative error of at most 0.009.
Values may be sent and summed in bfloat16 or wider, within the bound.
A program may use at most 64 MiB of HBM per device.

```python
import math
import jax
import jax.numpy as jnp
import numpy as np
from jax import lax

D = 8192
HD = 128
KVH = 4
QH = 32
TOK_DEV = 128
C = 512
TOKR = 4096
N_DP = 32
N_REPLICA = 16


def draw_queries(key, part):
    full_shape = (N_REPLICA, TOKR, QH * HD)
    drawn_values = jnp.clip(jax.random.normal(jax.random.fold_in(key, 1), full_shape, jnp.float32), -5.0, 5.0)
    return drawn_values.astype(jnp.bfloat16)


def draw_keys_in(key, part):
    full_shape = (N_REPLICA, TOKR, KVH * HD)
    drawn_values = jnp.clip(jax.random.normal(jax.random.fold_in(key, 2), full_shape, jnp.float32), -5.0, 5.0)
    return drawn_values.astype(jnp.bfloat16)


def set_ends(drawn, own_key, low, largest):
    longest = drawn.shape.index(max(drawn.shape))
    spots = []
    for shift in (0, 1):
        where = [jax.random.randint(jax.random.fold_in(own_key, axis), (), 0, length) for axis, length in enumerate(drawn.shape)]
        where[longest] = (where[longest] + shift) % drawn.shape[longest]
        spots.append(tuple(where))
    return drawn.at[spots[0]].set(low).at[spots[1]].set(largest)


def level_of(stream_key, extent, shards, low, top_value):
    def one(dim, shards_of):
        draws = jax.random.uniform(jax.random.fold_in(jax.random.fold_in(stream_key, 6), dim), (shards_of,), jnp.float32, low / len(shards), top_value / len(shards))
        return jnp.repeat(jnp.exp(draws), extent[dim] // shards_of).reshape((-1,) + (1,) * (len(extent) - dim - 1))

    factor_of = one(*shards[0])
    for cut in shards[1:]:
        factor_of = factor_of * one(*cut)
    return factor_of


def split_up(number_of, total, most, lean):
    portions = [(1 << 20) // math.isqrt(rank ** lean) + 1 for rank in range(2, number_of + 1)]
    spare, holding = total - most - (number_of - 1), [1] * (number_of - 1)
    while spare > 0:
        candidates = [i for i in range(number_of - 1) if holding[i] < most]
        pool, left = sum([portions[i] for i in candidates]), spare
        for i in candidates:
            addition = min(most - holding[i], max(1, left * portions[i] // pool), spare)
            holding[i] = holding[i] + addition
            spare = spare - addition
    return np.array([most] + holding)


def uneven(rng, count, total, limit, skew):
    if count == 2:
        one = jax.random.randint(rng, (), max(1, total - limit), min(limit, total - 1) + 1)
        return jnp.stack([one, total - one])
    tallies = jnp.asarray(split_up(count, total, limit, skew), jnp.int32)
    pairs = (count - 1) // 2
    source_of, receiver = tallies[1:1 + 2 * pairs:2], tallies[2:2 + 2 * pairs:2]
    room = jnp.minimum(source_of - 1, limit - receiver)
    passed = jax.random.randint(jax.random.fold_in(rng, 1), (pairs,), 0, 1 << 20) % (room + 1)
    tallies = tallies.at[1:1 + 2 * pairs:2].set(source_of - passed).at[2:2 + 2 * pairs:2].set(receiver + passed)
    return tallies[jax.random.permutation(jax.random.fold_in(rng, 2), count)]


def normal_values(own_key, dims, spread, limit, shards=(), kind=jnp.bfloat16):
    entries = spread * jax.random.normal(own_key, dims, jnp.float32)
    if shards:
        entries = entries * level_of(own_key, dims, shards, -0.22, 0.18)
    return jnp.clip(entries, -limit, limit).astype(kind)


def setup_inputs(seed: int = 0) -> dict:
    key_of = jax.random.split(jax.random.key(seed), 10)
    grad_parts = normal_values(key_of[0], (N_DP * N_DP, D // N_DP, C), 0.2, 1.1953125, ((0, 32), (1, 16)))
    master_weight = normal_values(key_of[1], (D, C), D ** -0.5, 0.0625, ((0, 512),), jnp.float32)
    moment_one = normal_values(key_of[2], (D, C), 0.3, 1.8, ((0, 512),), jnp.float32)
    moment_two = jnp.clip(jnp.exp(math.log(2.0) - 3.6888794 * jax.random.uniform(key_of[3], (D, C), jnp.float32) ** level_of(key_of[3], (D, C), ((0, 512),), -0.2, 0.2)), 0.05, 2.0)
    queries = draw_queries(jax.random.fold_in(key_of[9], 71), 0)
    keys_in = draw_keys_in(jax.random.fold_in(key_of[9], 71), 0)
    hidden = normal_values(key_of[6], (N_REPLICA, TOKR, D), 1.0, 6.0, ((0, 16), (1, 32)))
    segment_ids = jax.vmap(lambda own: jnp.searchsorted(jnp.cumsum(uneven(own, 2 * N_DP // 3, TOKR, 3 * TOK_DEV, 1)), jnp.arange(TOKR), side="right"))(jax.random.split(key_of[7], N_REPLICA)).reshape((N_REPLICA, TOKR)).astype(jnp.int32)
    packed_len = set_ends(jax.random.randint(key_of[8], (N_REPLICA,), TOKR // 2, TOKR + 1), jax.random.fold_in(key_of[8], 1), TOKR // 2, TOKR).astype(jnp.int32)
    return dict(grad_parts=grad_parts, master_weight=master_weight, moment_one=moment_one, moment_two=moment_two, queries=queries, keys_in=keys_in, hidden=hidden, segment_ids=segment_ids, packed_len=packed_len)


beta_one = 0.9
beta_two = 0.95
bias_one = 1.0 - 0.9 ** 10
bias_two = 1.0 - 0.95 ** 10
adam_eps = 1e-08
learn_rate = 0.002
weight_decay = 0.1

def replica_attention(query_rows, key_rows, value_rows, seg_rows, used_len):
    groups = QH // KVH
    block_count = query_rows.shape[0] // TOK_DEV
    padded_keys = jnp.concatenate([jnp.zeros((3 * TOK_DEV, KVH * HD), key_rows.dtype), key_rows], axis=0)
    padded_values = jnp.concatenate([jnp.zeros((3 * TOK_DEV, KVH * HD), value_rows.dtype), value_rows], axis=0)
    padded_segs = jnp.concatenate([jnp.full((3 * TOK_DEV,), -1, jnp.int32), seg_rows.astype(jnp.int32)], axis=0)

    def one_block(block_index):
        begin = (block_index * TOK_DEV).astype(jnp.int32)
        query_blk = lax.dynamic_slice_in_dim(query_rows, begin, TOK_DEV, 0).astype(jnp.float32)
        key_blk = lax.dynamic_slice_in_dim(padded_keys, begin, 4 * TOK_DEV, 0).astype(jnp.float32)
        value_blk = lax.dynamic_slice_in_dim(padded_values, begin, 4 * TOK_DEV, 0).astype(jnp.float32)
        seg_keys = lax.dynamic_slice_in_dim(padded_segs, begin, 4 * TOK_DEV, 0)
        seg_query = lax.dynamic_slice_in_dim(seg_rows.astype(jnp.int32), begin, TOK_DEV, 0)
        query_pos = begin + jnp.arange(TOK_DEV, dtype=jnp.int32)
        key_pos = begin - 3 * TOK_DEV + jnp.arange(4 * TOK_DEV, dtype=jnp.int32)
        allowed = (seg_query[:, None] == seg_keys[None, :]) & (key_pos[None, :] <= query_pos[:, None])
        query_heads = query_blk.reshape(TOK_DEV, KVH, groups, HD)
        key_heads = key_blk.reshape(4 * TOK_DEV, KVH, HD)
        value_heads = value_blk.reshape(4 * TOK_DEV, KVH, HD)
        scores = jnp.einsum('qhgd,khd->hgqk', query_heads, key_heads) * HD ** (-0.5)
        scores = jnp.where(allowed, scores, -jnp.inf)
        row_max = lax.optimization_barrier(jnp.max(scores, axis=-1, keepdims=True))
        weights = jnp.where(allowed, jnp.exp(scores - row_max), 0.0)
        totals = lax.optimization_barrier(jnp.sum(weights, axis=-1, keepdims=True))
        rounded = weights.astype(jnp.bfloat16)
        rounded = lax.optimization_barrier(rounded).astype(jnp.float32)
        mixed_out = jnp.einsum('hgqk,khd->qhgd', rounded, value_heads)
        mixed_out = mixed_out / jnp.transpose(totals, (2, 0, 1, 3))
        mixed_out = mixed_out.reshape(TOK_DEV, QH * HD)
        query_live = query_pos < used_len
        return jnp.where(query_live[:, None], mixed_out, 0.0).astype(jnp.bfloat16)
    blocks_out = lax.map(one_block, jnp.arange(block_count, dtype=jnp.int32))
    return blocks_out.reshape(block_count * TOK_DEV, QH * HD)

def reference(grad_parts, master_weight, moment_one, moment_two, queries, keys_in, hidden, segment_ids, packed_len):
    grad_total = lax.optimization_barrier(jnp.sum(grad_parts.astype(jnp.float32).reshape(N_DP, D, C), axis=0))
    new_first = beta_one * moment_one + (1.0 - beta_one) * grad_total
    new_second = beta_two * moment_two + (1.0 - beta_two) * grad_total * grad_total
    step_dir = new_first / bias_one / (jnp.sqrt(new_second / bias_two) + adam_eps) + weight_decay * master_weight
    new_master = master_weight - learn_rate * step_dir
    rollout_weight = new_master.astype(jnp.bfloat16)

    def per_replica(replica_items):
        query_rows, key_rows, hidden_rows, seg_rows, used_len = replica_items
        value_rows = jnp.dot(hidden_rows, rollout_weight, preferred_element_type=jnp.float32).astype(jnp.bfloat16)
        return replica_attention(query_rows, key_rows, value_rows, seg_rows, used_len)
    attended = lax.map(per_replica, (queries, keys_in, hidden, segment_ids, packed_len))
    return (new_master, new_first, new_second, attended)
```

```python
import functools

import jax
import jax.numpy as jnp
from jax import lax
from jax.experimental import pallas as pl
from jax.experimental.pallas import tpu as pltpu
from jax.sharding import PartitionSpec as P

HD = 128
NZ = 16
MESH = pl.DeviceIdType.MESH

beta_one = 0.9
beta_two = 0.95
bias_one = 1.0 - 0.9**10
bias_two = 1.0 - 0.95**10
adam_eps = 1e-08
learn_rate = 0.002
weight_decay = 0.1
LOG2E = 1.4426950408889634


def device_at(x, y, z, c):
    return (
        z * 2 + lax.div(x, jnp.int32(2)),
        y * 4 + lax.rem(x, jnp.int32(2)) * 2 + c,
    )


def wait_bytes(ref, sem):
    pltpu.make_async_copy(ref, ref, sem).wait()


def kernel(
    grad,
    master,
    moment_first,
    moment_second,
    queries,
    keys,
    hidden,
    segs,
    packed_len,
    master_out,
    first_out,
    second_out,
    attended,
    own_terms,
    pair_terms,
    pair_sums,
    z_terms,
    rounded,
    wbuf,
    hbuf,
    kbuf,
    segsrc,
    segbuf,
    bias,
    wts,
    tots,
    vout,
    vbuf,
    local_sem,
    send_sem,
    pair_sem,
    z_sem,
    hid_sem,
    key_sem,
    seg_sem,
    wz_sem,
    ring_sem,
    val_sem,
):
    i32 = jnp.int32
    dp = lax.axis_index("dp").astype(i32)
    rep = lax.axis_index("replica").astype(i32)
    z = lax.div(dp, i32(2))
    xh = lax.rem(dp, i32(2))
    y = lax.div(rep, i32(4))
    xl = lax.rem(lax.div(rep, i32(2)), i32(2))
    c = lax.rem(rep, i32(2))
    x = xh * 2 + xl

    def mod(value, n):
        return lax.rem(value + n, i32(n))

    def send(src, dst, s_sem, r_sem, device):
        copy = pltpu.make_async_remote_copy(
            src_ref=src,
            dst_ref=dst,
            send_sem=s_sem,
            recv_sem=r_sem,
            device_id=device,
            device_id_type=MESH,
        )
        copy.start()
        return copy

    hid_local = pltpu.make_async_copy(hidden, hbuf.at[c], local_sem.at[0])
    own_local = pltpu.make_async_copy(grad.at[:, xh], own_terms, local_sem.at[1])
    own_local.start()

    barrier = pltpu.get_barrier_semaphore()

    def greet(device):
        pl.semaphore_signal(barrier, inc=1, device_id=device, device_id_type=MESH)

    greet(device_at(mod(x + 2, 4), y, z, c))
    for step in (1, 3):
        greet(device_at(mod(x + step, 4), y, z, c))
        greet(device_at(x, mod(y + step, 4), z, c))

    def greet_z(d, carry):
        greet(device_at(x, y, mod(z + d, NZ), c))
        greet(device_at(x, y, mod(z + d, NZ), 1 - c))
        return carry

    lax.fori_loop(1, NZ, greet_z, 0)
    greet(device_at(x, y, z, 1 - c))
    other_x = mod(x + 2, 4)
    for shift in (1, 3, -1, -3):
        there = lax.div(mod(dp + shift, 32), i32(2))
        greet(device_at(other_x, y, there, 1 - c))
    for offset in (1, -1, 4 * xh - 2):
        greet(device_at(other_x, y, mod(z + offset, NZ), c))
    pl.semaphore_wait(barrier, 1 + 4 + 30 + 1 + 4 + 3)

    group_here = lax.div(z, i32(4))
    partner = device_at(other_x, y, z, c)
    order = (2, 1, 3, 0)
    for n, k in enumerate(order):
        g = mod(group_here + k, 4)
        rows = pl.ds(g * 4, 4)
        send(
            grad.at[rows, 1 - xh],
            pair_terms.at[rows],
            send_sem.at[0],
            pair_sem.at[n],
            partner,
        )

    sibling = device_at(x, y, z, 1 - c)
    hid_local.start()
    segsrc[...] = jnp.broadcast_to(segs[...], (8, 128))
    key_copies = []
    for o in (1, 2, 3):
        to = (mod(dp + o, 32), rep)
        key_copies.append(
            send(segsrc, segbuf.at[3 - o], seg_sem.at[3 + o - 1], seg_sem.at[o - 1], to)
        )
        key_copies.append(
            send(keys, kbuf.at[3 - o], key_sem.at[3 + o - 1], key_sem.at[o - 1], to)
        )
    hid_copy = send(hidden, hbuf.at[c], hid_sem.at[0], hid_sem.at[1], sibling)
    kbuf[3] = keys[...]
    segbuf[3] = segsrc[...]

    own_local.wait()
    for n, k in enumerate(order):
        g = mod(group_here + k, 4)
        rows = pl.ds(g * 4, 4)
        wait_bytes(pair_terms.at[rows], pair_sem.at[n])
        pair_sums[rows] = (
            own_terms[rows].astype(jnp.float32) + pair_terms[rows].astype(jnp.float32)
        ).astype(jnp.bfloat16)
        for i in range(1 if k == 0 else 0, 4):
            there = g * 4 + (mod(z + i, 4) if k == 0 else i)
            send(
                pair_sums.at[there],
                z_terms.at[z],
                send_sem.at[1],
                z_sem.at[0],
                device_at(x, y, there, c),
            )
    z_terms[z] = pair_sums[z]

    for copy in key_copies:
        copy.wait()
    seg_q = jnp.transpose(jnp.broadcast_to(segs[...], (128, 128)))
    row_id = lax.broadcasted_iota(i32, (128, 128), 0)
    col_id = lax.broadcasted_iota(i32, (128, 128), 1)
    for slot in range(4):
        o = 3 - slot
        same = seg_q == jnp.broadcast_to(segbuf[slot][0:1, :], (128, 128))
        if o == 0:
            allowed = same & (col_id <= row_id)
        else:
            allowed = same & (jnp.broadcast_to(dp, (128, 128)) >= o)
        bias[:, slot * 128 : (slot + 1) * 128] = jnp.where(allowed, 0.0, -1e30)

    def scores_of(head, carry):
        kv = lax.div(head, i32(8))
        q = queries[:, pl.ds(pl.multiple_of(head * HD, HD), HD)]
        k = kbuf[:, :, pl.ds(pl.multiple_of(kv * HD, HD), HD)].reshape(512, HD)
        s = lax.dot_general(
            q, k, (((1,), (1,)), ((), ())), preferred_element_type=jnp.float32
        )
        s = s + bias[...]
        top = jnp.max(s, axis=1, keepdims=True)
        w = jnp.exp2((s - top) * (HD**-0.5 * LOG2E))
        tots[head] = jnp.broadcast_to(jnp.sum(w, axis=1, keepdims=True), (128, HD))
        wts[head] = w.astype(jnp.bfloat16)
        return carry

    lax.fori_loop(0, 32, scores_of, 0)

    wait_bytes(z_terms.at[pl.ds(0, 15)], z_sem.at[0])
    grad_sum = jnp.sum(z_terms[...].astype(jnp.float32), axis=0)
    first_new = beta_one * moment_first[...] + (1.0 - beta_one) * grad_sum
    second_new = (
        beta_two * moment_second[...] + (1.0 - beta_two) * grad_sum * grad_sum
    )
    step_dir = (
        first_new / bias_one / (jnp.sqrt(second_new / bias_two) + adam_eps)
        + weight_decay * master[...]
    )
    master_new = master[...] - learn_rate * step_dir
    rows_new = master_new.astype(jnp.bfloat16)
    rounded[0] = rows_new[:, :256]
    rounded[1] = rows_new[:, 256:]

    own_rows = pl.ds(pl.multiple_of(c * 16, 16), 16)
    send(
        rounded.at[1 - c],
        wbuf.at[z, xh, y, xl, own_rows],
        send_sem.at[3],
        wz_sem.at[z],
        sibling,
    )
    for n, k in enumerate((0, 1, 3, 2)):
        g = mod(group_here + k, 4)
        for i in range(1 if k == 0 else 0, 4):
            there = g * 4 + (mod(z + i, 4) if k == 0 else i)
            send(
                rounded.at[c],
                wbuf.at[z, xh, y, xl, own_rows],
                send_sem.at[2],
                wz_sem.at[z],
                device_at(x, y, there, c),
            )
            send(
                rounded.at[1 - c],
                wbuf.at[z, xh, y, xl, own_rows],
                send_sem.at[3],
                wz_sem.at[z],
                device_at(x, y, there, 1 - c),
            )
    wbuf[z, xh, y, xl, own_rows] = rounded[c]
    master_out[...] = master_new
    first_out[...] = first_new
    second_out[...] = second_new

    near_x = (device_at(mod(x + 1, 4), y, z, c), device_at(mod(x + 3, 4), y, z, c))
    near_y = (device_at(x, mod(y + 1, 4), z, c), device_at(x, mod(y + 3, 4), z, c))

    def x_split(value):
        return lax.div(value, i32(2)), lax.rem(value, i32(2))

    gather_order = (0, 1, 3, 2)

    def group_of(n):
        return mod(group_here + gather_order[n], 4)

    def first_stage(n):
        g = group_of(n)
        if n == 0:
            wait_bytes(wbuf.at[z, xh, y, xl, pl.ds(0, 16)], wz_sem.at[z])
            for i in range(1, 4):
                zi = g * 4 + mod(z + i, 4)
                wait_bytes(wbuf.at[zi, xh, y, xl], wz_sem.at[zi])
        else:
            for i in range(4):
                zi = g * 4 + i
                wait_bytes(wbuf.at[zi, xh, y, xl], wz_sem.at[zi])
        for colour, near in ((0, near_x), (1, near_y)):
            part = wbuf.at[pl.ds(g * 4 + 2 * colour, 2), xh, y, xl]
            for way in (0, 1):
                send(part, part, send_sem.at[4], ring_sem.at[0, n, colour, way], near[way])

    def first_forward(n):
        g = group_of(n)
        for colour, near in ((0, near_x), (1, near_y)):
            for way in (0, 1):
                back = 3 if way == 0 else 1
                if colour == 0:
                    fh, fl = x_split(mod(x + back, 4))
                    fy = y
                else:
                    fh, fl, fy = xh, xl, mod(y + back, 4)
                zs = pl.ds(g * 4 + 2 * colour, 2)
                wait_bytes(wbuf.at[zs, fh, fy, fl], ring_sem.at[0, n, colour, way])
                part = wbuf.at[g * 4 + 2 * colour + way, fh, fy, fl]
                send(part, part, send_sem.at[5], ring_sem.at[1, n, colour, way], near[way])

    def second_stage(n):
        g = group_of(n)
        for colour, near in ((0, near_y), (1, near_x)):
            for way in (0, 1):
                if colour == 0:
                    fh, fl = x_split(mod(x + 2, 4))
                    fy = y
                else:
                    fh, fl, fy = xh, xl, mod(y + 2, 4)
                wait_bytes(
                    wbuf.at[g * 4 + 2 * colour + way, fh, fy, fl],
                    ring_sem.at[1, n, colour, way],
                )
            zs = pl.ds(g * 4 + 2 * colour, 2)
            part = wbuf.at[zs, :, y, :] if colour == 0 else wbuf.at[zs, xh, :, xl]
            for way in (0, 1):
                send(part, part, send_sem.at[6], ring_sem.at[2, n, colour, way], near[way])

    def second_forward(n):
        g = group_of(n)
        for colour, near in ((0, near_y), (1, near_x)):
            for way in (0, 1):
                back = 3 if way == 0 else 1
                zs = pl.ds(g * 4 + 2 * colour, 2)
                one = g * 4 + 2 * colour + way
                if colour == 0:
                    fy = mod(y + back, 4)
                    whole, part = wbuf.at[zs, :, fy, :], wbuf.at[one, :, fy, :]
                else:
                    fh, fl = x_split(mod(x + back, 4))
                    whole, part = wbuf.at[zs, fh, :, fl], wbuf.at[one, fh, :, fl]
                wait_bytes(whole, ring_sem.at[2, n, colour, way])
                send(part, part, send_sem.at[7], ring_sem.at[3, n, colour, way], near[way])

    def multiply(n, total):
        g = group_of(n)
        for colour in (0, 1):
            for way in (0, 1):
                one = g * 4 + 2 * colour + way
                if colour == 0:
                    part = wbuf.at[one, :, mod(y + 2, 4), :]
                else:
                    fh, fl = x_split(mod(x + 2, 4))
                    part = wbuf.at[one, fh, :, fl]
                wait_bytes(part, ring_sem.at[3, n, colour, way])

        def add(i, acc):
            zi = g * 4 + i
            cols = pl.ds(pl.multiple_of(zi * 512, 512), 512)
            return acc + jnp.dot(
                hbuf[:, :, cols].reshape(256, 512),
                wbuf[zi].reshape(512, 256),
                preferred_element_type=jnp.float32,
            )

        return lax.fori_loop(0, 4, add, total)

    total = jnp.zeros((256, 256), jnp.float32)
    for slot in range(8):
        if slot < 4:
            first_stage(slot)
        if 0 <= slot - 1 < 4:
            first_forward(slot - 1)
        if 0 <= slot - 2 < 4:
            second_stage(slot - 2)
        if 0 <= slot - 3 < 4:
            second_forward(slot - 3)
        if slot == 3:
            hid_local.wait()
            hid_copy.wait()
        if 0 <= slot - 4 < 4:
            total = multiply(slot - 4, total)

    vout[...] = total.astype(jnp.bfloat16).reshape(2, 128, 256)
    val_copies = []
    for o in (3, 2, 1, 0):
        there = mod(dp + o, 32)
        for other in (0, 1) if o else (1,):
            core = lax.rem(c + other, i32(2))
            val_copies.append(
                send(
                    vout.at[core],
                    vbuf.at[c, 3 - o],
                    val_sem.at[0, o, other],
                    val_sem.at[1, o, other],
                    (there, rep - c + core),
                )
            )
    vbuf[c, 3] = vout[c]

    wait_bytes(pair_terms, send_sem.at[0])
    wait_bytes(z_terms.at[pl.ds(0, 15)], send_sem.at[1])
    wait_bytes(wbuf.at[pl.ds(0, 15), 0, 0, 0, pl.ds(0, 16)], send_sem.at[2])
    wait_bytes(wbuf.at[pl.ds(0, 16), 0, 0, 0, pl.ds(0, 16)], send_sem.at[3])
    wait_bytes(wbuf.at[pl.ds(0, 2)], send_sem.at[4])
    wait_bytes(wbuf.at[pl.ds(0, 1)], send_sem.at[5])
    wait_bytes(wbuf.at[pl.ds(0, 8)], send_sem.at[6])
    wait_bytes(wbuf.at[pl.ds(0, 4)], send_sem.at[7])
    for copy in val_copies:
        copy.wait()

    pos = dp * 128 + lax.broadcasted_iota(i32, (128, HD), 0)
    live = pos < packed_len[0]
    for kv in range(4):
        v = vbuf[kv // 2, :, :, (kv % 2) * HD : (kv % 2 + 1) * HD].reshape(512, HD)

        def mix(j, carry):
            head = kv * 8 + j
            out = jnp.dot(wts[head], v, preferred_element_type=jnp.float32)
            out = jnp.where(live, out / tots[head], 0.0).astype(jnp.bfloat16)
            attended[:, pl.ds(pl.multiple_of(head * HD, HD), HD)] = out
            return carry

        lax.fori_loop(0, 8, mix, 0)


def on_device(
    grad_parts,
    master_weight,
    moment_one,
    moment_two,
    queries,
    keys_in,
    hidden,
    segment_ids,
    packed_len,
):
    bf16, f32 = jnp.bfloat16, jnp.float32
    any_spec = pl.BlockSpec(memory_space=pl.ANY)
    vmem = pl.BlockSpec(memory_space=pltpu.VMEM)
    smem = pl.BlockSpec(memory_space=pltpu.SMEM)
    dma = pltpu.SemaphoreType.DMA
    rows = jax.ShapeDtypeStruct((16, 512), f32)
    new_master, new_first, new_second, attended = pl.pallas_call(
        kernel,
        out_shape=(rows, rows, rows, jax.ShapeDtypeStruct((128, 4096), bf16)),
        in_specs=[any_spec, vmem, vmem, vmem, vmem, vmem, any_spec, vmem, smem],
        out_specs=(vmem, vmem, vmem, vmem),
        scratch_shapes=[
            pltpu.VMEM((NZ, 16, 512), bf16),
            pltpu.VMEM((NZ, 16, 512), bf16),
            pltpu.VMEM((NZ, 16, 512), bf16),
            pltpu.VMEM((NZ, 16, 512), bf16),
            pltpu.VMEM((2, 16, 256), bf16),
            pltpu.VMEM((NZ, 2, 4, 2, 32, 256), bf16),
            pltpu.VMEM((2, 128, 8192), bf16),
            pltpu.VMEM((4, 128, 512), bf16),
            pltpu.VMEM((8, 128), jnp.int32),
            pltpu.VMEM((4, 8, 128), jnp.int32),
            pltpu.VMEM((128, 512), f32),
            pltpu.VMEM((32, 128, 512), bf16),
            pltpu.VMEM((32, 128, HD), f32),
            pltpu.VMEM((2, 128, 256), bf16),
            pltpu.VMEM((2, 4, 128, 256), bf16),
            dma((2,)),
            dma((8,)),
            dma((4,)),
            dma((1,)),
            dma((2,)),
            dma((6,)),
            dma((6,)),
            dma((NZ,)),
            dma((4, 4, 2, 2)),
            dma((2, 4, 2)),
        ],
        compiler_params=pltpu.CompilerParams(
            collective_id=0, has_side_effects=True, vmem_limit_bytes=48 << 20
        ),
    )(
        grad_parts.reshape(NZ, 2, 16, 512),
        master_weight,
        moment_one,
        moment_two,
        queries[0],
        keys_in[0],
        hidden[0],
        segment_ids,
        packed_len,
    )
    return (new_master, new_first, new_second, attended[None])


def solution(mesh):
    in_specs = (
        P("dp", "replica", None),
        P(("dp", "replica"), None),
        P(("dp", "replica"), None),
        P(("dp", "replica"), None),
        P("replica", "dp", None),
        P("replica", "dp", None),
        P("replica", "dp", None),
        P("replica", "dp"),
        P("replica"),
    )
    out_specs = (
        P(("dp", "replica"), None),
        P(("dp", "replica"), None),
        P(("dp", "replica"), None),
        P("replica", "dp", None),
    )
    return jax.shard_map(
        on_device, mesh=mesh, in_specs=in_specs, out_specs=out_specs, check_vma=False
    )
```

```python
import jax
import jax.numpy as jnp
from jax import lax
from jax.experimental import pallas as pl
from jax.experimental.pallas import tpu as pltpu
from jax.sharding import PartitionSpec as P

HD = 128
NZ = 16
MESH = pl.DeviceIdType.MESH

beta_one = 0.9
beta_two = 0.95
bias_one = 1.0 - 0.9**10
bias_two = 1.0 - 0.95**10
adam_eps = 1e-08
learn_rate = 0.002
weight_decay = 0.1
LOG2E = 1.4426950408889634
UNROLL_S = 4
UNROLL_M = 8
UNROLL_W = 2
LAST = 3


def adam_update(grad_sum, master, moment_first, moment_second):
    first_new = beta_one * moment_first + (1.0 - beta_one) * grad_sum
    second_new = beta_two * moment_second + (1.0 - beta_two) * grad_sum * grad_sum
    step_dir = (
        first_new / bias_one / (jnp.sqrt(second_new / bias_two) + adam_eps)
        + weight_decay * master
    )
    master_new = master - learn_rate * step_dir
    return master_new, first_new, second_new, master_new.astype(jnp.bfloat16)


def device_at(x, y, z, c):
    return (
        z * 2 + lax.div(x, jnp.int32(2)),
        y * 4 + lax.rem(x, jnp.int32(2)) * 2 + c,
    )


def wait_bytes(ref, sem):
    pltpu.make_async_copy(ref, ref, sem).wait()


def kernel(
    grad,
    master_in,
    first_in,
    second_in,
    queries_in,
    keys_in,
    hidden,
    segs_in,
    packed_in,
    grad_out,
    attended,
    master,
    moment_first,
    moment_second,
    queries,
    segs,
    packed_len,
    own_terms,
    pair_terms,
    pair_sums,
    z_terms,
    rounded,
    wbuf,
    hbuf,
    kbuf,
    kpair,
    segsrc,
    segbuf,
    bias,
    wts,
    tots,
    vout,
    vbuf,
    local_sem,
    send_sem,
    pair_sem,
    z_sem,
    hid_sem,
    key_sem,
    seg_sem,
    wz_sem,
    ring_sem,
    val_sem,
):
    i32 = jnp.int32
    dp = lax.axis_index("dp").astype(i32)
    rep = lax.axis_index("replica").astype(i32)
    z = lax.div(dp, i32(2))
    xh = lax.rem(dp, i32(2))
    y = lax.div(rep, i32(4))
    xl = lax.rem(lax.div(rep, i32(2)), i32(2))
    c = lax.rem(rep, i32(2))
    x = xh * 2 + xl

    def mod(value, n):
        return lax.rem(value + n, i32(n))

    def send(src, dst, s_sem, r_sem, device):
        copy = pltpu.make_async_remote_copy(
            src_ref=src,
            dst_ref=dst,
            send_sem=s_sem,
            recv_sem=r_sem,
            device_id=device,
            device_id_type=MESH,
        )
        copy.start()
        return copy

    barrier = pltpu.get_barrier_semaphore()

    def greet(device):
        pl.semaphore_signal(barrier, inc=1, device_id=device, device_id_type=MESH)

    def greet_z(d, carry):
        greet(device_at(x, y, mod(z + d, NZ), c))
        greet(device_at(x, y, mod(z + d, NZ), 1 - c))
        return carry

    lax.fori_loop(1, NZ, greet_z, 0)
    sibling = device_at(x, y, z, 1 - c)
    other_x = mod(x + 2, 4)
    greet(sibling)
    for step in (1, 2, 3):
        greet(device_at(mod(x + step, 4), y, z, c))
        greet(device_at(x, mod(y + step, 4), z, c))
    for offset in (1, -1, 4 * xh - 2):
        greet(device_at(other_x, y, mod(z + offset, NZ), c))
    for offset in (0, 1, -1, 4 * xh - 2):
        greet(device_at(other_x, y, mod(z + offset, NZ), 1 - c))

    def local(n, src, dst):
        copy = pltpu.make_async_copy(src, dst, local_sem.at[n])
        copy.start()
        return copy

    own_local = local(0, grad.at[:, xh], own_terms)
    seg_local = local(1, segs_in, segs)
    state_local = (
        local(2, master_in, master),
        local(3, first_in, moment_first),
        local(4, second_in, moment_second),
    )
    late_local = (
        local(5, packed_in, packed_len),
        local(6, queries_in, queries),
        local(7, keys_in, kbuf.at[3]),
        local(8, hidden, hbuf.at[c]),
    )
    pl.semaphore_wait(barrier, 30 + 1 + 6 + 3 + 4)

    half_here = lax.div(z, i32(8))
    partner = device_at(other_x, y, z, c)

    def half_of(n):
        return lax.rem(half_here + n, i32(2))

    for p in (0, 1):
        for n in (1, 0):
            rows = pl.ds(half_of(n) * 8, 8)
            send(
                grad.at[rows, 1 - xh, :, pl.ds(p * 256, 256)],
                pair_terms.at[p, rows],
                send_sem.at[0],
                pair_sem.at[p, n],
                partner,
            )

    hid_copy = send(hidden, hbuf.at[c], hid_sem.at[0], hid_sem.at[1], sibling)
    pair_keys = send(keys_in, kpair, key_sem.at[4], key_sem.at[0], partner)
    seg_local.wait()
    segsrc[...] = jnp.broadcast_to(segs[...], (8, 128))
    segbuf[3] = segsrc[...]
    seg_copies = []
    for o in (1, 2, 3):
        seg_copies.append(
            send(
                segsrc,
                segbuf.at[3 - o],
                seg_sem.at[3 + o - 1],
                seg_sem.at[o - 1],
                (mod(dp + o, 32), rep),
            )
        )

    def z_partners(n):
        g = half_of(n)
        for i in range(1 if n == 0 else 0, 8):
            yield g * 8 + (lax.rem(z + i, i32(8)) if n == 0 else i)

    own_local.wait()
    for p in (0, 1):
        for n in (1, 0):
            rows = pl.ds(half_of(n) * 8, 8)
            wait_bytes(pair_terms.at[p, rows], pair_sem.at[p, n])
            own = own_terms[rows, :, p * 256 : (p + 1) * 256].astype(jnp.float32)
            pair_sums[p, rows] = (own + pair_terms[p, rows].astype(jnp.float32)).astype(
                jnp.bfloat16
            )
            for there in z_partners(n):
                send(
                    pair_sums.at[p, there],
                    z_terms.at[p, z],
                    send_sem.at[1],
                    z_sem.at[p],
                    device_at(x, y, there, c),
                )
        z_terms[p, z] = pair_sums[p, z]
    for copy in state_local:
        copy.wait()

    own_rows = pl.ds(pl.multiple_of(c * 16, 16), 16)

    def update(p):
        cols = slice(p * 256, (p + 1) * 256)
        wait_bytes(z_terms.at[p, pl.ds(0, 15)], z_sem.at[p])
        grad_sum = jnp.sum(z_terms[p].astype(jnp.float32), axis=0)
        rows_new = adam_update(
            grad_sum, master[:, cols], moment_first[:, cols], moment_second[:, cols]
        )[3]
        rounded[p, 0] = rows_new[:, :128]
        rounded[p, 1] = rows_new[:, 128:]
        mine = wbuf.at[p, z, xh, y, xl, own_rows]
        arrived = wz_sem.at[p, z]
        send(rounded.at[p, 1 - c], mine, send_sem.at[3], arrived, sibling)
        for n in (0, 1):
            for there in z_partners(n):
                to, across = device_at(x, y, there, c), device_at(x, y, there, 1 - c)
                send(rounded.at[p, c], mine, send_sem.at[2], arrived, to)
                send(rounded.at[p, 1 - c], mine, send_sem.at[3], arrived, across)
        wbuf[p, z, xh, y, xl, own_rows] = rounded[p, c]
        grad_out[:, cols] = grad_sum

    steps = (1, 3, 2)
    near_x = [device_at(mod(x + step, 4), y, z, c) for step in steps]
    near_y = [device_at(x, mod(y + step, 4), z, c) for step in steps]

    def x_split(value):
        return lax.div(value, i32(2)), lax.rem(value, i32(2))

    def four(n, colour):
        return pl.ds(half_of(n) * 8 + 4 * colour, 4)

    def two(n, colour, way):
        return pl.ds(half_of(n) * 8 + 4 * colour + 2 * way, 2)

    def column_at(colour, back):
        if colour == 0:
            fh, fl = x_split(mod(x + back, 4))
            return fh, y, fl
        return xh, mod(y + back, 4), xl

    def line_at(p, zs, colour, back):
        if colour == 0:
            return wbuf.at[p, zs, :, mod(y + back, 4), :]
        fh, fl = x_split(mod(x + back, 4))
        return wbuf.at[p, zs, fh, :, fl]

    def first_stage(r):
        p, n = r // 2, r % 2
        if n == 0:
            wait_bytes(wbuf.at[p, z, xh, y, xl, pl.ds(0, 16)], wz_sem.at[p, z])
        for zi in z_partners(n):
            wait_bytes(wbuf.at[p, zi, xh, y, xl], wz_sem.at[p, zi])
        for colour, near in ((0, near_x), (1, near_y)):
            part = wbuf.at[p, four(n, colour), xh, y, xl]
            for way in (2, 0, 1):
                send(part, part, send_sem.at[4], ring_sem.at[0, r, colour, way], near[way])

    def second_stage(r):
        p, n = r // 2, r % 2
        ways = (2, 0, 1) if r == LAST else (0, 1)
        for colour, near in ((0, near_y), (1, near_x)):
            for way in (0, 1, 2):
                fh, fy, fl = column_at(colour, 4 - steps[way])
                wait_bytes(
                    wbuf.at[p, four(n, colour), fh, fy, fl], ring_sem.at[0, r, colour, way]
                )
            part = line_at(p, four(n, colour), colour, 0)
            for way in ways:
                send(part, part, send_sem.at[5], ring_sem.at[1, r, colour, way], near[way])

    def second_forward(r):
        p, n = r // 2, r % 2
        for colour, near in ((0, near_y), (1, near_x)):
            for way in (0, 1):
                back = 4 - steps[way]
                wait_bytes(
                    line_at(p, four(n, colour), colour, back), ring_sem.at[1, r, colour, way]
                )
                part = line_at(p, two(n, colour, way), colour, back)
                send(part, part, send_sem.at[6], ring_sem.at[2, r, colour, way], near[way])

    def multiply(r, total):
        p, n = r // 2, r % 2
        for colour in (0, 1):
            if r == LAST:
                for way in (0, 1, 2):
                    wait_bytes(
                        line_at(p, four(n, colour), colour, 4 - steps[way]),
                        ring_sem.at[1, r, colour, way],
                    )
            else:
                for way in (0, 1):
                    wait_bytes(
                        line_at(p, two(n, colour, way), colour, 2),
                        ring_sem.at[2, r, colour, way],
                    )
        g = half_of(n)

        def add(i, acc):
            zi = g * 8 + i
            cols = pl.ds(pl.multiple_of(zi * 512, 512), 512)
            return acc + jnp.dot(
                hbuf[:, :, cols].reshape(256, 512),
                wbuf[p, zi].reshape(512, 128),
                preferred_element_type=jnp.float32,
            )

        return lax.fori_loop(0, 8, add, total, unroll=UNROLL_W)

    val_copies = ([], [])

    def send_values(p, total):
        vout[p] = total.astype(jnp.bfloat16).reshape(2, 128, 128)
        for o in (3, 2, 1, 0):
            for other in (0, 1) if o else (1,):
                core = lax.rem(c + other, i32(2))
                val_copies[p].append(
                    send(
                        vout.at[p, core],
                        vbuf.at[p, 3 - o, c],
                        val_sem.at[p, 0, o, other],
                        val_sem.at[p, 1, o, other],
                        (mod(dp + o, 32), rep - c + core),
                    )
                )
        vbuf[p, 3, c] = vout[p, c]

    def scores_of(head, carry):
        kv = lax.div(head, i32(8))
        q = queries[:, pl.ds(pl.multiple_of(head * HD, HD), HD)]
        k = kbuf[:, :, pl.ds(pl.multiple_of(kv * HD, HD), HD)].reshape(512, HD)
        s = lax.dot_general(
            q, k, (((1,), (1,)), ((), ())), preferred_element_type=jnp.float32
        )
        s = s + bias[...]
        top = jnp.max(s, axis=1, keepdims=True)
        w = jnp.exp2((s - top) * (HD**-0.5 * LOG2E))
        tots[head] = jnp.broadcast_to(jnp.sum(w, axis=1, keepdims=True), (128, HD))
        wts[head] = w.astype(jnp.bfloat16)
        return carry

    def scores(first, last):
        lax.fori_loop(first, last, scores_of, 0, unroll=UNROLL_S)

    def make_bias():
        for copy in seg_copies + key_copies:
            copy.wait()
        pair_keys.wait_send()

        @pl.when(xh == 0)
        def _():
            far_keys().wait()

        @pl.when(xh == 1)
        def _():
            kbuf[2] = kpair[...]

        seg_q = jnp.transpose(jnp.broadcast_to(segs[...], (128, 128)))
        row_id = lax.broadcasted_iota(i32, (128, 128), 0)
        col_id = lax.broadcasted_iota(i32, (128, 128), 1)
        for slot in range(4):
            o = 3 - slot
            same = seg_q == jnp.broadcast_to(segbuf[slot][0:1, :], (128, 128))
            if o == 0:
                allowed = same & (col_id <= row_id)
            else:
                allowed = same & (jnp.broadcast_to(dp, (128, 128)) >= o)
            bias[:, slot * 128 : (slot + 1) * 128] = jnp.where(allowed, 0.0, -1e30)

    def mix_heads(p):
        pos = dp * 128 + lax.broadcasted_iota(i32, (128, HD), 0)
        live = pos < packed_len[0]
        for core in (0, 1):
            v = vbuf[p, :, core].reshape(512, HD)

            def mix(j, carry):
                head = (2 * p + core) * 8 + j
                out = jnp.dot(wts[head], v, preferred_element_type=jnp.float32)
                out = jnp.where(live, out / tots[head], 0.0).astype(jnp.bfloat16)
                attended[:, pl.ds(pl.multiple_of(head * HD, HD), HD)] = out
                return carry

            lax.fori_loop(0, 8, mix, 0, unroll=UNROLL_M)

    key_copies = []

    def far_keys():
        return pltpu.make_async_remote_copy(
            src_ref=kpair,
            dst_ref=kbuf.at[0],
            send_sem=key_sem.at[7],
            recv_sem=key_sem.at[3],
            device_id=device_at(x, y, mod(z + 2, NZ), c),
            device_id_type=MESH,
        )

    def send_keys():
        pair_keys.wait_recv()
        next_z = device_at(x, y, mod(z + 1, NZ), c)

        @pl.when(xh == 0)
        def _():
            far_keys().start()

        key_copies.append(send(keys_in, kbuf.at[1], key_sem.at[5], key_sem.at[1], next_z))
        key_copies.append(
            send(kpair, kbuf.at[2 - 2 * xh], key_sem.at[6], key_sem.at[2], next_z)
        )

    zero = jnp.zeros((256, 128), jnp.float32)
    update(0)
    update(1)
    send_keys()
    first_stage(0)
    first_stage(1)
    second_stage(0)
    first_stage(2)
    second_stage(1)
    first_stage(3)
    for copy in late_local:
        copy.wait()
    hid_copy.wait()
    second_forward(0)
    second_stage(2)
    second_forward(1)
    total = multiply(0, zero)
    second_stage(3)
    total = multiply(1, total)
    send_values(0, total)
    second_forward(2)
    make_bias()
    scores(0, 8)
    total = multiply(2, zero)
    total = multiply(3, total)
    send_values(1, total)
    scores(8, 32)
    for copy in val_copies[0]:
        copy.wait()
    mix_heads(0)

    half = pl.ds(0, 16)
    wait_bytes(pair_terms, send_sem.at[0])
    wait_bytes(z_terms.at[:, pl.ds(0, 15)], send_sem.at[1])
    wait_bytes(wbuf.at[:, pl.ds(0, 15), 0, 0, 0, half], send_sem.at[2])
    wait_bytes(wbuf.at[:, :, 0, 0, 0, half], send_sem.at[3])
    wait_bytes(wbuf.at[0, pl.ds(0, 6)], send_sem.at[4])
    wait_bytes(wbuf.at[:, pl.ds(0, 9)], send_sem.at[5])
    wait_bytes(wbuf.at[0, pl.ds(0, 6)], send_sem.at[6])
    for copy in val_copies[1]:
        copy.wait()
    mix_heads(1)


def on_device(
    grad_parts,
    master_weight,
    moment_one,
    moment_two,
    queries,
    keys_in,
    hidden,
    segment_ids,
    packed_len,
):
    bf16, f32 = jnp.bfloat16, jnp.float32
    hbm = pl.BlockSpec(memory_space=pltpu.HBM)
    vmem = pl.BlockSpec(memory_space=pltpu.VMEM)
    dma = pltpu.SemaphoreType.DMA
    grad_sum, attended = pl.pallas_call(
        kernel,
        out_shape=(
            jax.ShapeDtypeStruct((16, 512), f32),
            jax.ShapeDtypeStruct((128, 4096), bf16),
        ),
        in_specs=[hbm] * 9,
        out_specs=(vmem, vmem),
        scratch_shapes=[
            pltpu.VMEM((16, 512), f32),
            pltpu.VMEM((16, 512), f32),
            pltpu.VMEM((16, 512), f32),
            pltpu.VMEM((128, 4096), bf16),
            pltpu.VMEM((1, 128), jnp.int32),
            pltpu.SMEM((1,), jnp.int32),
            pltpu.VMEM((NZ, 16, 512), bf16),
            pltpu.VMEM((2, NZ, 16, 256), bf16),
            pltpu.VMEM((2, NZ, 16, 256), bf16),
            pltpu.VMEM((2, NZ, 16, 256), bf16),
            pltpu.VMEM((2, 2, 16, 128), bf16),
            pltpu.VMEM((2, NZ, 2, 4, 2, 32, 128), bf16),
            pltpu.VMEM((2, 128, 8192), bf16),
            pltpu.VMEM((4, 128, 512), bf16),
            pltpu.VMEM((128, 512), bf16),
            pltpu.VMEM((8, 128), jnp.int32),
            pltpu.VMEM((4, 8, 128), jnp.int32),
            pltpu.VMEM((128, 512), f32),
            pltpu.VMEM((32, 128, 512), bf16),
            pltpu.VMEM((32, 128, HD), f32),
            pltpu.VMEM((2, 2, 128, 128), bf16),
            pltpu.VMEM((2, 4, 2, 128, 128), bf16),
            dma((9,)),
            dma((8,)),
            dma((2, 2)),
            dma((2,)),
            dma((2,)),
            dma((8,)),
            dma((6,)),
            dma((2, NZ)),
            dma((3, 4, 2, 3)),
            dma((2, 2, 4, 2)),
        ],
        compiler_params=pltpu.CompilerParams(
            collective_id=0, has_side_effects=True, vmem_limit_bytes=64 << 20
        ),
    )(
        grad_parts.reshape(NZ, 2, 16, 512),
        master_weight,
        moment_one,
        moment_two,
        queries[0],
        keys_in[0],
        hidden[0],
        segment_ids,
        packed_len,
    )
    new_master, new_first, new_second, _ = adam_update(
        grad_sum, master_weight, moment_one, moment_two
    )
    return (new_master, new_first, new_second, attended[None])


def solution(mesh):
    in_specs = (
        P("dp", "replica", None),
        P(("dp", "replica"), None),
        P(("dp", "replica"), None),
        P(("dp", "replica"), None),
        P("replica", "dp", None),
        P("replica", "dp", None),
        P("replica", "dp", None),
        P("replica", "dp"),
        P("replica"),
    )
    out_specs = (
        P(("dp", "replica"), None),
        P(("dp", "replica"), None),
        P(("dp", "replica"), None),
        P("replica", "dp", None),
    )
    return jax.shard_map(
        on_device, mesh=mesh, in_specs=in_specs, out_specs=out_specs, check_vma=False
    )
```

```python
import jax
import jax.numpy as jnp
from jax import lax
from jax.experimental import pallas as pl
from jax.experimental.pallas import tpu as pltpu
from jax.sharding import PartitionSpec as P

HD = 128
NZ = 16
MESH = pl.DeviceIdType.MESH

beta_one = 0.9
beta_two = 0.95
bias_one = 1.0 - 0.9**10
bias_two = 1.0 - 0.95**10
adam_eps = 1e-08
learn_rate = 0.002
weight_decay = 0.1
LOG2E = 1.4426950408889634
UNROLL_S = 4
UNROLL_M = 8


def adam_update(grad_sum, master, moment_first, moment_second):
    first_new = beta_one * moment_first + (1.0 - beta_one) * grad_sum
    second_new = beta_two * moment_second + (1.0 - beta_two) * grad_sum * grad_sum
    step_dir = (
        first_new / bias_one / (jnp.sqrt(second_new / bias_two) + adam_eps)
        + weight_decay * master
    )
    master_new = master - learn_rate * step_dir
    return master_new, first_new, second_new, master_new.astype(jnp.bfloat16)


def device_at(x, y, z, c):
    return (
        z * 2 + lax.div(x, jnp.int32(2)),
        y * 4 + lax.rem(x, jnp.int32(2)) * 2 + c,
    )


def wait_bytes(ref, sem):
    pltpu.make_async_copy(ref, ref, sem).wait()


def kernel(
    grad,
    master_in,
    first_in,
    second_in,
    queries_in,
    keys_in,
    hidden,
    segs_in,
    packed_in,
    grad_out,
    attended,
    master,
    moment_first,
    moment_second,
    queries,
    segs,
    packed_len,
    own_terms,
    pair_terms,
    pair_sums,
    z_terms,
    rounded,
    wbuf,
    hset,
    kbuf,
    kpair,
    segsrc,
    segbuf,
    bias,
    wts,
    tots,
    parts,
    gathered,
    vbuf,
    local_sem,
    send_sem,
    pair_sem,
    z_sem,
    hid_sem,
    key_sem,
    seg_sem,
    wz_sem,
    ring_sem,
    part_sem,
    val_sem,
):
    i32 = jnp.int32
    dp = lax.axis_index("dp").astype(i32)
    rep = lax.axis_index("replica").astype(i32)
    z = lax.div(dp, i32(2))
    xh = lax.rem(dp, i32(2))
    y = lax.div(rep, i32(4))
    xl = lax.rem(lax.div(rep, i32(2)), i32(2))
    c = lax.rem(rep, i32(2))
    x = xh * 2 + xl

    def mod(value, n):
        return lax.rem(value + n, i32(n))

    def send(src, dst, s_sem, r_sem, device):
        copy = pltpu.make_async_remote_copy(
            src_ref=src,
            dst_ref=dst,
            send_sem=s_sem,
            recv_sem=r_sem,
            device_id=device,
            device_id_type=MESH,
        )
        copy.start()
        return copy

    barrier = pltpu.get_barrier_semaphore()

    def greet(device):
        pl.semaphore_signal(barrier, inc=1, device_id=device, device_id_type=MESH)

    def greet_z(d, carry):
        greet(device_at(x, y, mod(z + d, NZ), c))
        return carry

    lax.fori_loop(1, NZ, greet_z, 0)
    other_x = mod(x + 2, 4)
    for step in (1, 2, 3):
        greet(device_at(mod(x + step, 4), y, z, c))
    for offset in (1, -1, 4 * xh - 2):
        greet(device_at(other_x, y, mod(z + offset, NZ), c))

    def member(k):
        if k == 7:
            return y, 1 - c
        return mod(y + (2, 1, 3)[k // 2], 4), lax.rem(c + k % 2, i32(2))

    members = [member(k) for k in (0, 1, 2, 3, 4, 5, 7)]
    for my, mc in members:
        greet(device_at(x, my, z, mc))
    plane = 4 * c + y
    for source in (plane, plane + 8):

        @pl.when(source != z)
        def _():
            def greet_plane(n, carry):
                greet(device_at(x, lax.div(n, i32(2)), source, lax.rem(n, i32(2))))
                return carry

            lax.fori_loop(0, 8, greet_plane, 0)

    def local(n, src, dst):
        copy = pltpu.make_async_copy(src, dst, local_sem.at[n])
        copy.start()
        return copy

    own_local = local(0, grad.at[:, xh], own_terms)
    seg_local = local(1, segs_in, segs)
    state_local = (
        local(2, master_in, master),
        local(3, first_in, moment_first),
        local(4, second_in, moment_second),
    )
    late_local = (
        local(5, packed_in, packed_len),
        local(6, queries_in, queries),
        local(7, keys_in, kbuf.at[3]),
    )
    pl.semaphore_wait(barrier, 15 + 3 + 3 + 7 + 15)

    half_here = lax.div(z, i32(8))
    partner = device_at(other_x, y, z, c)

    def half_of(n):
        return lax.rem(half_here + n, i32(2))

    for p in (0, 1):
        for n in (1, 0):
            rows = pl.ds(half_of(n) * 8, 8)
            send(
                grad.at[rows, 1 - xh, :, pl.ds(p * 256, 256)],
                pair_terms.at[p, rows],
                send_sem.at[0],
                pair_sem.at[p, n],
                partner,
            )

    next_z = device_at(x, y, mod(z + 1, NZ), c)
    key_copies = [send(keys_in, kbuf.at[1], key_sem.at[5], key_sem.at[1], next_z)]
    pair_keys = send(keys_in, kpair, key_sem.at[4], key_sem.at[0], partner)

    me = y * 2 + c
    for my, mc in members:
        for n in (0, 1):
            cols = pl.ds(pl.multiple_of((4 * mc + my + 8 * n) * 512, 512), 512)
            send(
                hidden.at[:, cols],
                hset.at[n, me],
                hid_sem.at[0],
                hid_sem.at[1],
                device_at(x, my, z, mc),
            )
    for n in (0, 1):
        cols = pl.ds(pl.multiple_of((plane + 8 * n) * 512, 512), 512)
        pltpu.make_async_copy(hidden.at[:, cols], hset.at[n, me], hid_sem.at[1]).start()

    seg_local.wait()
    segsrc[...] = jnp.broadcast_to(segs[...], (8, 128))
    segbuf[3] = segsrc[...]
    seg_copies = []
    for o in (1, 2, 3):
        seg_copies.append(
            send(
                segsrc,
                segbuf.at[3 - o],
                seg_sem.at[3 + o - 1],
                seg_sem.at[o - 1],
                (mod(dp + o, 32), rep),
            )
        )

    def z_partners(n):
        g = half_of(n)
        for i in range(1 if n == 0 else 0, 8):
            yield g * 8 + (lax.rem(z + i, i32(8)) if n == 0 else i)

    own_local.wait()
    for p in (0, 1):
        for n in (1, 0):
            rows = pl.ds(half_of(n) * 8, 8)
            wait_bytes(pair_terms.at[p, rows], pair_sem.at[p, n])
            own = own_terms[rows, :, p * 256 : (p + 1) * 256].astype(jnp.float32)
            pair_sums[p, rows] = (own + pair_terms[p, rows].astype(jnp.float32)).astype(
                jnp.bfloat16
            )
            for there in z_partners(n):
                send(
                    pair_sums.at[p, there],
                    z_terms.at[p, z],
                    send_sem.at[1],
                    z_sem.at[p],
                    device_at(x, y, there, c),
                )
        z_terms[p, z] = pair_sums[p, z]
    for copy in state_local:
        copy.wait()

    def update(p):
        cols = slice(p * 256, (p + 1) * 256)
        wait_bytes(z_terms.at[p, pl.ds(0, 15)], z_sem.at[p])
        grad_sum = jnp.sum(z_terms[p].astype(jnp.float32), axis=0)
        rows_new = adam_update(
            grad_sum, master[:, cols], moment_first[:, cols], moment_second[:, cols]
        )[3]
        rounded[p] = rows_new
        side = lax.div(z, i32(8))
        mine = wbuf.at[p, side, xh, y, xl, c]
        ty, tc = lax.rem(z, i32(4)), lax.rem(lax.div(z, i32(4)), i32(2))

        def send_z(d, carry):
            send(
                rounded.at[p],
                mine,
                send_sem.at[2],
                wz_sem.at[p],
                device_at(x, ty, mod(z + d, NZ), tc),
            )
            return carry

        lax.fori_loop(1, NZ, send_z, 0)
        here = (ty == y) & (tc == c)

        @pl.when(here)
        def _():
            pltpu.make_async_copy(rounded.at[p], mine, wz_sem.at[p]).start()

        @pl.when(jnp.logical_not(here))
        def _():
            send(rounded.at[p], mine, send_sem.at[3 + p], wz_sem.at[p], device_at(x, ty, z, tc))

        grad_out[:, cols] = grad_sum

    def column(p, back):
        source = mod(x + back, 4)
        return wbuf.at[p, :, lax.div(source, i32(2)), :, lax.rem(source, i32(2))]

    def gather_x(p):
        part = column(p, 0)
        wait_bytes(part, wz_sem.at[p])
        for n, step in enumerate((2, 1, 3)):
            send(
                part,
                part,
                send_sem.at[5],
                ring_sem.at[p, n],
                device_at(mod(x + step, 4), y, z, c),
            )

    def multiply(p):
        for n, step in enumerate((2, 1, 3)):
            wait_bytes(column(p, 4 - step), ring_sem.at[p, n])

        def product(k, carry):
            pair = pl.ds(k * 2, 2)
            acc = jnp.dot(
                hset[0, pair].reshape(256, 512),
                wbuf[p, 0].reshape(512, 256),
                preferred_element_type=jnp.float32,
            )
            acc = acc + jnp.dot(
                hset[1, pair].reshape(256, 512),
                wbuf[p, 1].reshape(512, 256),
                preferred_element_type=jnp.float32,
            )
            parts[p, pair] = acc.astype(jnp.bfloat16).reshape(2, 128, 256)
            return carry

        lax.fori_loop(0, 4, product, 0)
        for my, mc in members:
            send(
                parts.at[p, my * 2 + mc],
                gathered.at[p, me],
                send_sem.at[6],
                part_sem.at[p],
                device_at(x, my, z, mc),
            )
        gathered[p, me] = parts[p, me]

    val_copies = ([], [])

    def send_values(p):
        wait_bytes(gathered.at[p, pl.ds(0, 7)], part_sem.at[p])
        total = jnp.sum(gathered[p].astype(jnp.float32), axis=0)
        vbuf[p, 3] = total.astype(jnp.bfloat16)
        for o in (3, 2, 1):
            val_copies[p].append(
                send(
                    vbuf.at[p, 3],
                    vbuf.at[p, 3 - o],
                    val_sem.at[p, 0, o],
                    val_sem.at[p, 1, o],
                    (mod(dp + o, 32), rep),
                )
            )

    def scores_of(head, carry):
        kv = lax.div(head, i32(8))
        q = queries[:, pl.ds(pl.multiple_of(head * HD, HD), HD)]
        k = kbuf[:, :, pl.ds(pl.multiple_of(kv * HD, HD), HD)].reshape(512, HD)
        s = lax.dot_general(
            q, k, (((1,), (1,)), ((), ())), preferred_element_type=jnp.float32
        )
        s = s + bias[...]
        top = jnp.max(s, axis=1, keepdims=True)
        w = jnp.exp2((s - top) * (HD**-0.5 * LOG2E))
        tots[head] = jnp.broadcast_to(jnp.sum(w, axis=1, keepdims=True), (128, HD))
        wts[head] = w.astype(jnp.bfloat16)
        return carry

    def scores(first, last):
        lax.fori_loop(first, last, scores_of, 0, unroll=UNROLL_S)

    def make_bias():
        for copy in seg_copies + key_copies:
            copy.wait()
        pair_keys.wait_send()

        @pl.when(xh == 0)
        def _():
            far_keys().wait()

        @pl.when(xh == 1)
        def _():
            kbuf[2] = kpair[...]

        seg_q = jnp.transpose(jnp.broadcast_to(segs[...], (128, 128)))
        row_id = lax.broadcasted_iota(i32, (128, 128), 0)
        col_id = lax.broadcasted_iota(i32, (128, 128), 1)
        for slot in range(4):
            o = 3 - slot
            same = seg_q == jnp.broadcast_to(segbuf[slot][0:1, :], (128, 128))
            if o == 0:
                allowed = same & (col_id <= row_id)
            else:
                allowed = same & (jnp.broadcast_to(dp, (128, 128)) >= o)
            bias[:, slot * 128 : (slot + 1) * 128] = jnp.where(allowed, 0.0, -1e30)

    def mix_heads(p):
        pos = dp * 128 + lax.broadcasted_iota(i32, (128, HD), 0)
        live = pos < packed_len[0]
        for core in (0, 1):
            v = vbuf[p, :, :, core * HD : (core + 1) * HD].reshape(512, HD)

            def mix(j, carry):
                head = (2 * p + core) * 8 + j
                out = jnp.dot(wts[head], v, preferred_element_type=jnp.float32)
                out = jnp.where(live, out / tots[head], 0.0).astype(jnp.bfloat16)
                attended[:, pl.ds(pl.multiple_of(head * HD, HD), HD)] = out
                return carry

            lax.fori_loop(0, 8, mix, 0, unroll=UNROLL_M)

    def far_keys():
        return pltpu.make_async_remote_copy(
            src_ref=kpair,
            dst_ref=kbuf.at[0],
            send_sem=key_sem.at[7],
            recv_sem=key_sem.at[3],
            device_id=device_at(x, y, mod(z + 2, NZ), c),
            device_id_type=MESH,
        )

    def send_keys():
        pair_keys.wait_recv()
        @pl.when(xh == 0)
        def _():
            far_keys().start()

        key_copies.append(
            send(kpair, kbuf.at[2 - 2 * xh], key_sem.at[6], key_sem.at[2], next_z)
        )

    update(0)
    update(1)
    send_keys()
    gather_x(0)
    gather_x(1)
    wait_bytes(hset, hid_sem.at[1])
    multiply(0)
    for copy in late_local:
        copy.wait()
    make_bias()
    scores(0, 8)
    multiply(1)
    send_values(0)
    scores(8, 32)
    send_values(1)
    for copy in val_copies[0]:
        copy.wait()
    mix_heads(0)

    wait_bytes(pair_terms, send_sem.at[0])
    wait_bytes(z_terms.at[:, pl.ds(0, 15)], send_sem.at[1])
    wait_bytes(z_terms.at[:, pl.ds(0, 15)], send_sem.at[2])
    here = (lax.rem(z, i32(4)) == y) & (lax.rem(lax.div(z, i32(4)), i32(2)) == c)

    @pl.when(jnp.logical_not(here))
    def _():
        wait_bytes(rounded.at[0], send_sem.at[3])
        wait_bytes(rounded.at[1], send_sem.at[4])

    wait_bytes(wbuf.at[:, :, :, pl.ds(0, 3)], send_sem.at[5])
    wait_bytes(parts.at[:, pl.ds(0, 7)], send_sem.at[6])
    wait_bytes(hset.at[:, pl.ds(0, 7)], hid_sem.at[0])
    for copy in val_copies[1]:
        copy.wait()
    mix_heads(1)


def on_device(
    grad_parts,
    master_weight,
    moment_one,
    moment_two,
    queries,
    keys_in,
    hidden,
    segment_ids,
    packed_len,
):
    bf16, f32 = jnp.bfloat16, jnp.float32
    hbm = pl.BlockSpec(memory_space=pltpu.HBM)
    vmem = pl.BlockSpec(memory_space=pltpu.VMEM)
    dma = pltpu.SemaphoreType.DMA
    grad_sum, attended = pl.pallas_call(
        kernel,
        out_shape=(
            jax.ShapeDtypeStruct((16, 512), f32),
            jax.ShapeDtypeStruct((128, 4096), bf16),
        ),
        in_specs=[hbm] * 9,
        out_specs=(vmem, vmem),
        scratch_shapes=[
            pltpu.VMEM((16, 512), f32),
            pltpu.VMEM((16, 512), f32),
            pltpu.VMEM((16, 512), f32),
            pltpu.VMEM((128, 4096), bf16),
            pltpu.VMEM((1, 128), jnp.int32),
            pltpu.SMEM((1,), jnp.int32),
            pltpu.VMEM((NZ, 16, 512), bf16),
            pltpu.VMEM((2, NZ, 16, 256), bf16),
            pltpu.VMEM((2, NZ, 16, 256), bf16),
            pltpu.VMEM((2, NZ, 16, 256), bf16),
            pltpu.VMEM((2, 16, 256), bf16),
            pltpu.VMEM((2, 2, 2, 4, 2, 2, 16, 256), bf16),
            pltpu.VMEM((2, 8, 128, 512), bf16),
            pltpu.VMEM((4, 128, 512), bf16),
            pltpu.VMEM((128, 512), bf16),
            pltpu.VMEM((8, 128), jnp.int32),
            pltpu.VMEM((4, 8, 128), jnp.int32),
            pltpu.VMEM((128, 512), f32),
            pltpu.VMEM((32, 128, 512), bf16),
            pltpu.VMEM((32, 128, HD), f32),
            pltpu.VMEM((2, 8, 128, 256), bf16),
            pltpu.VMEM((2, 8, 128, 256), bf16),
            pltpu.VMEM((2, 4, 128, 256), bf16),
            dma((8,)),
            dma((8,)),
            dma((2, 2)),
            dma((2,)),
            dma((2,)),
            dma((8,)),
            dma((6,)),
            dma((2,)),
            dma((2, 3)),
            dma((2,)),
            dma((2, 2, 4)),
        ],
        compiler_params=pltpu.CompilerParams(
            collective_id=0, has_side_effects=True, vmem_limit_bytes=64 << 20
        ),
    )(
        grad_parts.reshape(NZ, 2, 16, 512),
        master_weight,
        moment_one,
        moment_two,
        queries[0],
        keys_in[0],
        hidden[0],
        segment_ids,
        packed_len,
    )
    new_master, new_first, new_second, _ = adam_update(
        grad_sum, master_weight, moment_one, moment_two
    )
    return (new_master, new_first, new_second, attended[None])


def solution(mesh):
    in_specs = (
        P("dp", "replica", None),
        P(("dp", "replica"), None),
        P(("dp", "replica"), None),
        P(("dp", "replica"), None),
        P("replica", "dp", None),
        P("replica", "dp", None),
        P("replica", "dp", None),
        P("replica", "dp"),
        P("replica"),
    )
    out_specs = (
        P(("dp", "replica"), None),
        P(("dp", "replica"), None),
        P(("dp", "replica"), None),
        P("replica", "dp", None),
    )
    return jax.shard_map(
        on_device, mesh=mesh, in_specs=in_specs, out_specs=out_specs, check_vma=False
    )
```

```python
import jax
import jax.numpy as jnp
from jax import lax
from jax.experimental import pallas as pl
from jax.experimental.pallas import tpu as pltpu
from jax.sharding import PartitionSpec as P

HD = 128
NZ = 16
MESH = pl.DeviceIdType.MESH

beta_one = 0.9
beta_two = 0.95
bias_one = 1.0 - 0.9**10
bias_two = 1.0 - 0.95**10
adam_eps = 1e-08
learn_rate = 0.002
weight_decay = 0.1
LOG2E = 1.4426950408889634
UNROLL_S = 4
UNROLL_M = 8


def adam_update(grad_sum, master, moment_first, moment_second):
    first_new = beta_one * moment_first + (1.0 - beta_one) * grad_sum
    second_new = beta_two * moment_second + (1.0 - beta_two) * grad_sum * grad_sum
    step_dir = (
        first_new / bias_one / (jnp.sqrt(second_new / bias_two) + adam_eps)
        + weight_decay * master
    )
    master_new = master - learn_rate * step_dir
    return master_new, first_new, second_new, master_new.astype(jnp.bfloat16)


def device_at(x, y, z, c):
    return (
        z * 2 + lax.div(x, jnp.int32(2)),
        y * 4 + lax.rem(x, jnp.int32(2)) * 2 + c,
    )


def wait_bytes(ref, sem):
    pltpu.make_async_copy(ref, ref, sem).wait()


def kernel(
    grad,
    master_in,
    first_in,
    second_in,
    queries_in,
    keys_in,
    hidden,
    segs_in,
    packed_in,
    grad_out,
    attended,
    master,
    moment_first,
    moment_second,
    queries,
    segs,
    packed_len,
    own_terms,
    pair_terms,
    pair_sums,
    z_terms,
    rounded,
    wbuf,
    hset,
    kbuf,
    kpair,
    segsrc,
    segbuf,
    bias,
    wts,
    tots,
    parts,
    gathered,
    vbuf,
    local_sem,
    send_sem,
    pair_sem,
    z_sem,
    hid_sem,
    key_sem,
    seg_sem,
    wz_sem,
    ring_sem,
    part_sem,
    val_sem,
):
    i32 = jnp.int32
    dp = lax.axis_index("dp").astype(i32)
    rep = lax.axis_index("replica").astype(i32)
    z = lax.div(dp, i32(2))
    xh = lax.rem(dp, i32(2))
    y = lax.div(rep, i32(4))
    xl = lax.rem(lax.div(rep, i32(2)), i32(2))
    c = lax.rem(rep, i32(2))
    x = xh * 2 + xl

    def mod(value, n):
        return lax.rem(value + n, i32(n))

    def send(src, dst, s_sem, r_sem, device):
        copy = pltpu.make_async_remote_copy(
            src_ref=src,
            dst_ref=dst,
            send_sem=s_sem,
            recv_sem=r_sem,
            device_id=device,
            device_id_type=MESH,
        )
        copy.start()
        return copy

    barrier = pltpu.get_barrier_semaphore()

    def greet(device):
        pl.semaphore_signal(barrier, inc=1, device_id=device, device_id_type=MESH)

    def greet_z(d, carry):
        greet(device_at(x, y, mod(z + d, NZ), c))
        return carry

    lax.fori_loop(1, NZ, greet_z, 0)
    other_x = mod(x + 2, 4)
    for step in (1, 2, 3):
        greet(device_at(mod(x + step, 4), y, z, c))
    for offset in (1, -1, 4 * xh - 2):
        greet(device_at(other_x, y, mod(z + offset, NZ), c))

    def member(k):
        if k == 7:
            return y, 1 - c
        return mod(y + (2, 1, 3)[k // 2], 4), lax.rem(c + k % 2, i32(2))

    members = [member(k) for k in (0, 1, 2, 3, 4, 5, 7)]
    for my, mc in members:
        greet(device_at(x, my, z, mc))
    plane = 4 * c + y
    for source in (plane, plane + 8):

        @pl.when(source != z)
        def _():
            def greet_plane(n, carry):
                greet(device_at(x, lax.div(n, i32(2)), source, lax.rem(n, i32(2))))
                return carry

            lax.fori_loop(0, 8, greet_plane, 0)

    def local(n, src, dst):
        copy = pltpu.make_async_copy(src, dst, local_sem.at[n])
        copy.start()
        return copy

    own_local = local(0, grad.at[:, xh], own_terms)
    seg_local = local(1, segs_in, segs)
    state_local = (
        local(2, master_in, master),
        local(3, first_in, moment_first),
        local(4, second_in, moment_second),
    )
    late_local = (
        local(5, packed_in, packed_len),
        local(6, queries_in, queries),
        local(7, keys_in, kbuf.at[3]),
    )
    pl.semaphore_wait(barrier, 15 + 3 + 3 + 7 + 15)

    half_here = lax.div(z, i32(8))
    partner = device_at(other_x, y, z, c)

    def half_of(n):
        return lax.rem(half_here + n, i32(2))

    for p in (0, 1):
        for n in (1, 0):
            rows = pl.ds(half_of(n) * 8, 8)
            send(
                grad.at[rows, 1 - xh, :, pl.ds(p * 256, 256)],
                pair_terms.at[p, rows],
                send_sem.at[0],
                pair_sem.at[p, n],
                partner,
            )

    next_z = device_at(x, y, mod(z + 1, NZ), c)
    key_copies = [send(keys_in, kbuf.at[1], key_sem.at[5], key_sem.at[1], next_z)]
    pair_keys = send(keys_in, kpair, key_sem.at[4], key_sem.at[0], partner)

    me = y * 2 + c
    for my, mc in members:
        for n in (0, 1):
            cols = pl.ds(pl.multiple_of((4 * mc + my + 8 * n) * 512, 512), 512)
            send(
                hidden.at[:, cols],
                hset.at[n, me],
                hid_sem.at[0],
                hid_sem.at[1],
                device_at(x, my, z, mc),
            )
    for n in (0, 1):
        cols = pl.ds(pl.multiple_of((plane + 8 * n) * 512, 512), 512)
        pltpu.make_async_copy(hidden.at[:, cols], hset.at[n, me], hid_sem.at[1]).start()

    seg_local.wait()
    segsrc[...] = jnp.broadcast_to(segs[...], (8, 128))
    segbuf[3] = segsrc[...]
    seg_copies = []
    for o in (1, 2, 3):
        seg_copies.append(
            send(
                segsrc,
                segbuf.at[3 - o],
                seg_sem.at[3 + o - 1],
                seg_sem.at[o - 1],
                (mod(dp + o, 32), rep),
            )
        )

    def z_partners(n):
        g = half_of(n)
        for i in range(1 if n == 0 else 0, 8):
            yield g * 8 + (lax.rem(z + i, i32(8)) if n == 0 else i)

    own_local.wait()
    for p in (0, 1):
        for n in (1, 0):
            rows = pl.ds(half_of(n) * 8, 8)
            wait_bytes(pair_terms.at[p, rows], pair_sem.at[p, n])
            own = own_terms[rows, :, p * 256 : (p + 1) * 256].astype(jnp.float32)
            pair_sums[p, rows] = (own + pair_terms[p, rows].astype(jnp.float32)).astype(
                jnp.bfloat16
            )
            for there in z_partners(n):
                send(
                    pair_sums.at[p, there],
                    z_terms.at[p, z],
                    send_sem.at[1],
                    z_sem.at[p],
                    device_at(x, y, there, c),
                )
        z_terms[p, z] = pair_sums[p, z]
    for copy in state_local:
        copy.wait()

    def update(p):
        cols = slice(p * 256, (p + 1) * 256)
        wait_bytes(z_terms.at[p, pl.ds(0, 15)], z_sem.at[p])
        grad_sum = jnp.sum(z_terms[p].astype(jnp.float32), axis=0)
        rows_new = adam_update(
            grad_sum, master[:, cols], moment_first[:, cols], moment_second[:, cols]
        )[3]
        ty, tc = lax.rem(z, i32(4)), lax.rem(lax.div(z, i32(4)), i32(2))
        here = (ty == y) & (tc == c)
        for q in (2 * p, 2 * p + 1):
            rounded[q] = rows_new[:, (q % 2) * HD : (q % 2 + 1) * HD]
            mine = wbuf.at[q, lax.div(z, i32(8)), xh, y, xl, c]

            def send_z(d, carry):
                send(
                    rounded.at[q],
                    mine,
                    send_sem.at[2],
                    wz_sem.at[q],
                    device_at(x, ty, mod(z + d, NZ), tc),
                )
                return carry

            lax.fori_loop(1, NZ, send_z, 0)

            @pl.when(here)
            def _():
                pltpu.make_async_copy(rounded.at[q], mine, wz_sem.at[q]).start()

            @pl.when(jnp.logical_not(here))
            def _():
                send(
                    rounded.at[q],
                    mine,
                    send_sem.at[8 + q],
                    wz_sem.at[q],
                    device_at(x, ty, z, tc),
                )

        grad_out[:, cols] = grad_sum

    def column(q, back):
        source = mod(x + back, 4)
        return wbuf.at[q, :, lax.div(source, i32(2)), :, lax.rem(source, i32(2))]

    def gather_x(q):
        part = column(q, 0)
        wait_bytes(part, wz_sem.at[q])
        for n, step in enumerate((2, 1, 3)):
            send(
                part,
                part,
                send_sem.at[5],
                ring_sem.at[q, n],
                device_at(mod(x + step, 4), y, z, c),
            )

    def multiply(q):
        for n, step in enumerate((2, 1, 3)):
            wait_bytes(column(q, 4 - step), ring_sem.at[q, n])

        def product(k, carry):
            pair = pl.ds(k * 2, 2)
            acc = jnp.dot(
                hset[0, pair].reshape(256, 512),
                wbuf[q, 0].reshape(512, HD),
                preferred_element_type=jnp.float32,
            )
            acc = acc + jnp.dot(
                hset[1, pair].reshape(256, 512),
                wbuf[q, 1].reshape(512, HD),
                preferred_element_type=jnp.float32,
            )
            parts[q, pair] = acc.astype(jnp.bfloat16).reshape(2, 128, HD)
            return carry

        lax.fori_loop(0, 4, product, 0, unroll=2)
        for my, mc in members:
            send(
                parts.at[q, my * 2 + mc],
                gathered.at[q, me],
                send_sem.at[6],
                part_sem.at[q],
                device_at(x, my, z, mc),
            )
        gathered[q, me] = parts[q, me]

    val_copies = ([], [], [], [])

    def send_values(q):
        wait_bytes(gathered.at[q, pl.ds(0, 7)], part_sem.at[q])
        total = jnp.sum(gathered[q].astype(jnp.float32), axis=0)
        vbuf[q, 3] = total.astype(jnp.bfloat16)
        for o in (3, 2, 1):
            val_copies[q].append(
                send(
                    vbuf.at[q, 3],
                    vbuf.at[q, 3 - o],
                    val_sem.at[q, 0, o],
                    val_sem.at[q, 1, o],
                    (mod(dp + o, 32), rep),
                )
            )

    def scores_of(head, carry):
        kv = lax.div(head, i32(8))
        q = queries[:, pl.ds(pl.multiple_of(head * HD, HD), HD)]
        k = kbuf[:, :, pl.ds(pl.multiple_of(kv * HD, HD), HD)].reshape(512, HD)
        s = lax.dot_general(
            q, k, (((1,), (1,)), ((), ())), preferred_element_type=jnp.float32
        )
        s = s + bias[...]
        top = jnp.max(s, axis=1, keepdims=True)
        w = jnp.exp2((s - top) * (HD**-0.5 * LOG2E))
        tots[head] = jnp.broadcast_to(jnp.sum(w, axis=1, keepdims=True), (128, HD))
        wts[head] = w.astype(jnp.bfloat16)
        return carry

    def scores(first, last):
        lax.fori_loop(first, last, scores_of, 0, unroll=UNROLL_S)

    def make_bias():
        for copy in seg_copies:
            copy.wait()
        key_copies[0].wait()
        key_copies[1].wait_send()
        pair_keys.wait_send()

        @pl.when(xh == 0)
        def _():
            far_keys().wait()

        @pl.when(xh == 1)
        def _():
            kbuf[2] = kpair[...]

        seg_q = jnp.transpose(jnp.broadcast_to(segs[...], (128, 128)))
        row_id = lax.broadcasted_iota(i32, (128, 128), 0)
        col_id = lax.broadcasted_iota(i32, (128, 128), 1)
        for slot in range(4):
            o = 3 - slot
            same = seg_q == jnp.broadcast_to(segbuf[slot][0:1, :], (128, 128))
            if o == 0:
                allowed = same & (col_id <= row_id)
            else:
                allowed = same & (jnp.broadcast_to(dp, (128, 128)) >= o)
            bias[:, slot * 128 : (slot + 1) * 128] = jnp.where(allowed, 0.0, -1e30)

    def mix_heads(q):
        for copy in val_copies[q]:
            copy.wait()
        pos = dp * 128 + lax.broadcasted_iota(i32, (128, HD), 0)
        live = pos < packed_len[0]
        v = vbuf[q].reshape(512, HD)

        def mix(j, carry):
            head = q * 8 + j
            out = jnp.dot(wts[head], v, preferred_element_type=jnp.float32)
            out = jnp.where(live, out / tots[head], 0.0).astype(jnp.bfloat16)
            attended[:, pl.ds(pl.multiple_of(head * HD, HD), HD)] = out
            return carry

        lax.fori_loop(0, 8, mix, 0, unroll=UNROLL_M)

    def far_keys():
        return pltpu.make_async_remote_copy(
            src_ref=kbuf.at[2],
            dst_ref=kbuf.at[0],
            send_sem=key_sem.at[7],
            recv_sem=key_sem.at[3],
            device_id=next_z,
            device_id_type=MESH,
        )

    def send_keys():
        pair_keys.wait_recv()
        key_copies.append(
            send(kpair, kbuf.at[2 - 2 * xh], key_sem.at[6], key_sem.at[2], next_z)
        )

    def forward_keys():
        key_copies[1].wait_recv()

        @pl.when(xh == 0)
        def _():
            far_keys().start()

    update(0)
    update(1)
    gather_x(0)
    gather_x(1)
    gather_x(2)
    send_keys()
    wait_bytes(hset, hid_sem.at[1])
    multiply(0)
    gather_x(3)
    multiply(1)
    send_values(0)
    multiply(2)
    send_values(1)
    forward_keys()
    multiply(3)
    send_values(2)
    for copy in late_local:
        copy.wait()
    make_bias()
    scores(0, 8)
    send_values(3)
    scores(8, 32)
    mix_heads(0)
    mix_heads(1)
    mix_heads(2)

    wait_bytes(pair_terms, send_sem.at[0])
    wait_bytes(z_terms.at[:, pl.ds(0, 15)], send_sem.at[1])
    wait_bytes(z_terms.at[:, pl.ds(0, 15)], send_sem.at[2])
    here = (lax.rem(z, i32(4)) == y) & (lax.rem(lax.div(z, i32(4)), i32(2)) == c)

    @pl.when(jnp.logical_not(here))
    def _():
        for q in range(4):
            wait_bytes(rounded.at[q], send_sem.at[8 + q])

    wait_bytes(wbuf.at[:, :, :, pl.ds(0, 3)], send_sem.at[5])
    wait_bytes(parts.at[:, pl.ds(0, 7)], send_sem.at[6])
    wait_bytes(hset.at[:, pl.ds(0, 7)], hid_sem.at[0])
    mix_heads(3)


def on_device(
    grad_parts,
    master_weight,
    moment_one,
    moment_two,
    queries,
    keys_in,
    hidden,
    segment_ids,
    packed_len,
):
    bf16, f32 = jnp.bfloat16, jnp.float32
    hbm = pl.BlockSpec(memory_space=pltpu.HBM)
    vmem = pl.BlockSpec(memory_space=pltpu.VMEM)
    dma = pltpu.SemaphoreType.DMA
    grad_sum, attended = pl.pallas_call(
        kernel,
        out_shape=(
            jax.ShapeDtypeStruct((16, 512), f32),
            jax.ShapeDtypeStruct((128, 4096), bf16),
        ),
        in_specs=[hbm] * 9,
        out_specs=(vmem, vmem),
        scratch_shapes=[
            pltpu.VMEM((16, 512), f32),
            pltpu.VMEM((16, 512), f32),
            pltpu.VMEM((16, 512), f32),
            pltpu.VMEM((128, 4096), bf16),
            pltpu.VMEM((1, 128), jnp.int32),
            pltpu.SMEM((1,), jnp.int32),
            pltpu.VMEM((NZ, 16, 512), bf16),
            pltpu.VMEM((2, NZ, 16, 256), bf16),
            pltpu.VMEM((2, NZ, 16, 256), bf16),
            pltpu.VMEM((2, NZ, 16, 256), bf16),
            pltpu.VMEM((4, 16, HD), bf16),
            pltpu.VMEM((4, 2, 2, 4, 2, 2, 16, HD), bf16),
            pltpu.VMEM((2, 8, 128, 512), bf16),
            pltpu.VMEM((4, 128, 512), bf16),
            pltpu.VMEM((128, 512), bf16),
            pltpu.VMEM((8, 128), jnp.int32),
            pltpu.VMEM((4, 8, 128), jnp.int32),
            pltpu.VMEM((128, 512), f32),
            pltpu.VMEM((32, 128, 512), bf16),
            pltpu.VMEM((32, 128, HD), f32),
            pltpu.VMEM((4, 8, 128, HD), bf16),
            pltpu.VMEM((4, 8, 128, HD), bf16),
            pltpu.VMEM((4, 4, 128, HD), bf16),
            dma((8,)),
            dma((12,)),
            dma((2, 2)),
            dma((2,)),
            dma((2,)),
            dma((8,)),
            dma((6,)),
            dma((4,)),
            dma((4, 3)),
            dma((4,)),
            dma((4, 2, 4)),
        ],
        compiler_params=pltpu.CompilerParams(
            collective_id=0, has_side_effects=True, vmem_limit_bytes=64 << 20
        ),
    )(
        grad_parts.reshape(NZ, 2, 16, 512),
        master_weight,
        moment_one,
        moment_two,
        queries[0],
        keys_in[0],
        hidden[0],
        segment_ids,
        packed_len,
    )
    new_master, new_first, new_second, _ = adam_update(
        grad_sum, master_weight, moment_one, moment_two
    )
    return (new_master, new_first, new_second, attended[None])


def solution(mesh):
    in_specs = (
        P("dp", "replica", None),
        P(("dp", "replica"), None),
        P(("dp", "replica"), None),
        P(("dp", "replica"), None),
        P("replica", "dp", None),
        P("replica", "dp", None),
        P("replica", "dp", None),
        P("replica", "dp"),
        P("replica"),
    )
    out_specs = (
        P(("dp", "replica"), None),
        P(("dp", "replica"), None),
        P(("dp", "replica"), None),
        P("replica", "dp", None),
    )
    return jax.shard_map(
        on_device, mesh=mesh, in_specs=in_specs, out_specs=out_specs, check_vma=False
    )
```

```python
import jax
import jax.numpy as jnp
from jax import lax
from jax.experimental import pallas as pl
from jax.experimental.pallas import tpu as pltpu
from jax.sharding import PartitionSpec as P

HD = 128
NZ = 16
MESH = pl.DeviceIdType.MESH

beta_one = 0.9
beta_two = 0.95
bias_one = 1.0 - 0.9**10
bias_two = 1.0 - 0.95**10
adam_eps = 1e-08
learn_rate = 0.002
weight_decay = 0.1
LOG2E = 1.4426950408889634
UNROLL_S = 4
UNROLL_M = 8


def adam_update(grad_sum, master, moment_first, moment_second):
    first_new = beta_one * moment_first + (1.0 - beta_one) * grad_sum
    second_new = beta_two * moment_second + (1.0 - beta_two) * grad_sum * grad_sum
    step_dir = (
        first_new / bias_one / (jnp.sqrt(second_new / bias_two) + adam_eps)
        + weight_decay * master
    )
    master_new = master - learn_rate * step_dir
    return master_new, first_new, second_new, master_new.astype(jnp.bfloat16)


def device_at(x, y, z, c):
    return (
        z * 2 + lax.div(x, jnp.int32(2)),
        y * 4 + lax.rem(x, jnp.int32(2)) * 2 + c,
    )


def wait_bytes(ref, sem):
    pltpu.make_async_copy(ref, ref, sem).wait()


def kernel(
    grad,
    master_in,
    first_in,
    second_in,
    queries_in,
    keys_in,
    hidden,
    segs_in,
    packed_in,
    grad_out,
    attended,
    master,
    moment_first,
    moment_second,
    queries,
    segs,
    packed_len,
    own_terms,
    pair_terms,
    pair_sums,
    z_terms,
    rounded,
    wbuf,
    hset,
    kbuf,
    kpair,
    segsrc,
    segbuf,
    bias,
    wts,
    tots,
    parts,
    gathered,
    vbuf,
    local_sem,
    send_sem,
    pair_sem,
    z_sem,
    hid_sem,
    key_sem,
    seg_sem,
    wz_sem,
    ring_sem,
    part_sem,
    val_sem,
):
    i32 = jnp.int32
    dp = lax.axis_index("dp").astype(i32)
    rep = lax.axis_index("replica").astype(i32)
    z = lax.div(dp, i32(2))
    xh = lax.rem(dp, i32(2))
    y = lax.div(rep, i32(4))
    xl = lax.rem(lax.div(rep, i32(2)), i32(2))
    c = lax.rem(rep, i32(2))
    x = xh * 2 + xl

    def mod(value, n):
        return lax.rem(value + n, i32(n))

    def send(src, dst, s_sem, r_sem, device):
        copy = pltpu.make_async_remote_copy(
            src_ref=src,
            dst_ref=dst,
            send_sem=s_sem,
            recv_sem=r_sem,
            device_id=device,
            device_id_type=MESH,
        )
        copy.start()
        return copy

    barrier = pltpu.get_barrier_semaphore()

    def greet(device):
        pl.semaphore_signal(barrier, inc=1, device_id=device, device_id_type=MESH)

    def greet_z(d, carry):
        greet(device_at(x, y, mod(z + d, NZ), c))
        return carry

    lax.fori_loop(1, NZ, greet_z, 0)
    other_x = mod(x + 2, 4)
    for step in (1, 2, 3):
        greet(device_at(mod(x + step, 4), y, z, c))
    for offset in (1, -1, 4 * xh - 2):
        greet(device_at(other_x, y, mod(z + offset, NZ), c))

    def member(k):
        if k == 7:
            return y, 1 - c
        return mod(y + (2, 1, 3)[k // 2], 4), lax.rem(c + k % 2, i32(2))

    members = [member(k) for k in (0, 1, 2, 3, 4, 5, 7)]
    for my, mc in members:
        greet(device_at(x, my, z, mc))
    plane = 4 * c + y
    for source in (plane, plane + 8):

        @pl.when(source != z)
        def _():
            def greet_plane(n, carry):
                greet(device_at(x, lax.div(n, i32(2)), source, lax.rem(n, i32(2))))
                return carry

            lax.fori_loop(0, 8, greet_plane, 0)

    def local(n, src, dst):
        copy = pltpu.make_async_copy(src, dst, local_sem.at[n])
        copy.start()
        return copy

    own_local = local(0, grad.at[:, xh], own_terms)
    seg_local = local(1, segs_in, segs)
    state_local = (
        local(2, master_in, master),
        local(3, first_in, moment_first),
        local(4, second_in, moment_second),
    )
    late_local = (
        local(5, packed_in, packed_len),
        local(6, queries_in, queries),
        local(7, keys_in, kbuf.at[3]),
    )
    pl.semaphore_wait(barrier, 15 + 3 + 3 + 7 + 15)

    half_here = lax.div(z, i32(8))
    partner = device_at(other_x, y, z, c)

    def half_of(n):
        return lax.rem(half_here + n, i32(2))

    for p in (0, 1):
        for n in (1, 0):
            rows = pl.ds(half_of(n) * 8, 8)
            send(
                grad.at[rows, 1 - xh, :, pl.ds(p * 256, 256)],
                pair_terms.at[p, rows],
                send_sem.at[0],
                pair_sem.at[p, n],
                partner,
            )

    next_z = device_at(x, y, mod(z + 1, NZ), c)
    key_copies = [send(keys_in, kbuf.at[1], key_sem.at[5], key_sem.at[1], next_z)]
    pair_keys = send(keys_in, kpair, key_sem.at[4], key_sem.at[0], partner)

    me = y * 2 + c
    for my, mc in members:
        for n in (0, 1):
            cols = pl.ds(pl.multiple_of((4 * mc + my + 8 * n) * 512, 512), 512)
            send(
                hidden.at[:, cols],
                hset.at[n, me],
                hid_sem.at[0],
                hid_sem.at[1],
                device_at(x, my, z, mc),
            )
    for n in (0, 1):
        cols = pl.ds(pl.multiple_of((plane + 8 * n) * 512, 512), 512)
        pltpu.make_async_copy(hidden.at[:, cols], hset.at[n, me], hid_sem.at[1]).start()

    seg_local.wait()
    segsrc[...] = jnp.broadcast_to(segs[...], (8, 128))
    segbuf[3] = segsrc[...]
    seg_copies = []
    for o in (1, 2, 3):
        seg_copies.append(
            send(
                segsrc,
                segbuf.at[3 - o],
                seg_sem.at[3 + o - 1],
                seg_sem.at[o - 1],
                (mod(dp + o, 32), rep),
            )
        )

    def z_partners(n):
        g = half_of(n)
        for i in range(1 if n == 0 else 0, 8):
            yield g * 8 + (lax.rem(z + i, i32(8)) if n == 0 else i)

    own_local.wait()
    for p in (0, 1):
        for n in (1, 0):
            rows = pl.ds(half_of(n) * 8, 8)
            wait_bytes(pair_terms.at[p, rows], pair_sem.at[p, n])
            own = own_terms[rows, :, p * 256 : (p + 1) * 256].astype(jnp.float32)
            pair_sums[p, rows] = (own + pair_terms[p, rows].astype(jnp.float32)).astype(
                jnp.bfloat16
            )
            for there in z_partners(n):
                send(
                    pair_sums.at[p, there],
                    z_terms.at[p, z],
                    send_sem.at[1],
                    z_sem.at[p],
                    device_at(x, y, there, c),
                )
        z_terms[p, z] = pair_sums[p, z]
    for copy in state_local:
        copy.wait()

    def update(p):
        cols = slice(p * 256, (p + 1) * 256)
        wait_bytes(z_terms.at[p, pl.ds(0, 15)], z_sem.at[p])
        grad_sum = jnp.sum(z_terms[p].astype(jnp.float32), axis=0)
        rows_new = adam_update(
            grad_sum, master[:, cols], moment_first[:, cols], moment_second[:, cols]
        )[3]
        ty, tc = lax.rem(z, i32(4)), lax.rem(lax.div(z, i32(4)), i32(2))
        here = (ty == y) & (tc == c)
        for q in (2 * p, 2 * p + 1):
            rounded[q] = rows_new[:, (q % 2) * HD : (q % 2 + 1) * HD]
            mine = wbuf.at[q, lax.div(z, i32(8)), xh, y, xl, c]

            def send_z(d, carry):
                send(
                    rounded.at[q],
                    mine,
                    send_sem.at[2],
                    wz_sem.at[q],
                    device_at(x, ty, mod(z + d, NZ), tc),
                )
                return carry

            lax.fori_loop(1, NZ, send_z, 0)

            @pl.when(here)
            def _():
                pltpu.make_async_copy(rounded.at[q], mine, wz_sem.at[q]).start()

            @pl.when(jnp.logical_not(here))
            def _():
                send(
                    rounded.at[q],
                    mine,
                    send_sem.at[8 + q],
                    wz_sem.at[q],
                    device_at(x, ty, z, tc),
                )

        grad_out[:, cols] = grad_sum

    def column(q, back):
        source = mod(x + back, 4)
        return wbuf.at[q, :, lax.div(source, i32(2)), :, lax.rem(source, i32(2))]

    def gather_x(q):
        part = column(q, 0)
        wait_bytes(part, wz_sem.at[q])
        for n, step in enumerate((2, 1, 3)):
            send(
                part,
                part,
                send_sem.at[5],
                ring_sem.at[q, n],
                device_at(mod(x + step, 4), y, z, c),
            )

    def multiply(q):
        for n, step in enumerate((2, 1, 3)):
            wait_bytes(column(q, 4 - step), ring_sem.at[q, n])

        def product(k, carry):
            pair = pl.ds(k * 2, 2)
            acc = jnp.dot(
                hset[0, pair].reshape(256, 512),
                wbuf[q, 0].reshape(512, HD),
                preferred_element_type=jnp.float32,
            )
            acc = acc + jnp.dot(
                hset[1, pair].reshape(256, 512),
                wbuf[q, 1].reshape(512, HD),
                preferred_element_type=jnp.float32,
            )
            parts[q, pair] = acc.astype(jnp.bfloat16).reshape(2, 128, HD)
            return carry

        lax.fori_loop(0, 4, product, 0, unroll=2)
        for my, mc in members:
            send(
                parts.at[q, my * 2 + mc],
                gathered.at[q, me],
                send_sem.at[6],
                part_sem.at[q],
                device_at(x, my, z, mc),
            )
        gathered[q, me] = parts[q, me]

    val_copies = ([], [], [], [])

    def send_values(q):
        wait_bytes(gathered.at[q, pl.ds(0, 7)], part_sem.at[q])
        total = jnp.sum(gathered[q].astype(jnp.float32), axis=0)
        vbuf[q, 3] = total.astype(jnp.bfloat16)
        for o in (3, 2, 1):
            val_copies[q].append(
                send(
                    vbuf.at[q, 3],
                    vbuf.at[q, 3 - o],
                    val_sem.at[q, 0, o],
                    val_sem.at[q, 1, o],
                    (mod(dp + o, 32), rep),
                )
            )

    def scores_of(head, carry):
        kv = lax.div(head, i32(8))
        q = queries[:, pl.ds(pl.multiple_of(head * HD, HD), HD)]
        k = kbuf[:, :, pl.ds(pl.multiple_of(kv * HD, HD), HD)].reshape(512, HD)
        s = lax.dot_general(
            q, k, (((1,), (1,)), ((), ())), preferred_element_type=jnp.float32
        )
        s = s + bias[...]
        top = jnp.max(s, axis=1, keepdims=True)
        w = jnp.exp2((s - top) * (HD**-0.5 * LOG2E))
        tots[head] = jnp.broadcast_to(jnp.sum(w, axis=1, keepdims=True), (128, HD))
        wts[head] = w.astype(jnp.bfloat16)
        return carry

    def scores(first, last):
        lax.fori_loop(first, last, scores_of, 0, unroll=UNROLL_S)

    def make_bias():
        for copy in seg_copies:
            copy.wait()
        key_copies[0].wait()
        key_copies[1].wait_send()
        pair_keys.wait_send()

        @pl.when(xh == 0)
        def _():
            far_keys().wait()

        @pl.when(xh == 1)
        def _():
            kbuf[2] = kpair[...]

        seg_q = jnp.transpose(jnp.broadcast_to(segs[...], (128, 128)))
        row_id = lax.broadcasted_iota(i32, (128, 128), 0)
        col_id = lax.broadcasted_iota(i32, (128, 128), 1)
        for slot in range(4):
            o = 3 - slot
            same = seg_q == jnp.broadcast_to(segbuf[slot][0:1, :], (128, 128))
            if o == 0:
                allowed = same & (col_id <= row_id)
            else:
                allowed = same & (jnp.broadcast_to(dp, (128, 128)) >= o)
            bias[:, slot * 128 : (slot + 1) * 128] = jnp.where(allowed, 0.0, -1e30)

    def mix_heads(q):
        for copy in val_copies[q]:
            copy.wait()
        pos = dp * 128 + lax.broadcasted_iota(i32, (128, HD), 0)
        live = pos < packed_len[0]
        v = vbuf[q].reshape(512, HD)

        def mix(j, carry):
            head = q * 8 + j
            out = jnp.dot(wts[head], v, preferred_element_type=jnp.float32)
            out = jnp.where(live, out / tots[head], 0.0).astype(jnp.bfloat16)
            attended[:, pl.ds(pl.multiple_of(head * HD, HD), HD)] = out
            return carry

        lax.fori_loop(0, 8, mix, 0, unroll=UNROLL_M)

    def far_keys():
        return pltpu.make_async_remote_copy(
            src_ref=kbuf.at[2],
            dst_ref=kbuf.at[0],
            send_sem=key_sem.at[7],
            recv_sem=key_sem.at[3],
            device_id=next_z,
            device_id_type=MESH,
        )

    def send_keys():
        pair_keys.wait_recv()
        key_copies.append(
            send(kpair, kbuf.at[2 - 2 * xh], key_sem.at[6], key_sem.at[2], next_z)
        )

    def forward_keys():
        key_copies[1].wait_recv()

        @pl.when(xh == 0)
        def _():
            far_keys().start()

    update(0)
    update(1)
    gather_x(0)
    gather_x(1)
    send_keys()
    gather_x(2)
    wait_bytes(hset, hid_sem.at[1])
    multiply(0)
    gather_x(3)
    forward_keys()
    multiply(1)
    multiply(2)
    send_values(0)
    multiply(3)
    send_values(1)
    send_values(2)
    for copy in late_local:
        copy.wait()
    make_bias()
    scores(0, 8)
    send_values(3)
    scores(8, 32)
    mix_heads(0)
    mix_heads(1)
    mix_heads(2)

    wait_bytes(pair_terms, send_sem.at[0])
    wait_bytes(z_terms.at[:, pl.ds(0, 15)], send_sem.at[1])
    wait_bytes(z_terms.at[:, pl.ds(0, 15)], send_sem.at[2])
    here = (lax.rem(z, i32(4)) == y) & (lax.rem(lax.div(z, i32(4)), i32(2)) == c)

    @pl.when(jnp.logical_not(here))
    def _():
        for q in range(4):
            wait_bytes(rounded.at[q], send_sem.at[8 + q])

    wait_bytes(wbuf.at[:, :, :, pl.ds(0, 3)], send_sem.at[5])
    wait_bytes(parts.at[:, pl.ds(0, 7)], send_sem.at[6])
    wait_bytes(hset.at[:, pl.ds(0, 7)], hid_sem.at[0])
    mix_heads(3)


def on_device(
    grad_parts,
    master_weight,
    moment_one,
    moment_two,
    queries,
    keys_in,
    hidden,
    segment_ids,
    packed_len,
):
    bf16, f32 = jnp.bfloat16, jnp.float32
    hbm = pl.BlockSpec(memory_space=pltpu.HBM)
    vmem = pl.BlockSpec(memory_space=pltpu.VMEM)
    dma = pltpu.SemaphoreType.DMA
    grad_sum, attended = pl.pallas_call(
        kernel,
        out_shape=(
            pltpu.VMEM((16, 512), f32),
            pltpu.VMEM((128, 4096), bf16),
        ),
        in_specs=[hbm] * 9,
        out_specs=(vmem, vmem),
        scratch_shapes=[
            pltpu.VMEM((16, 512), f32),
            pltpu.VMEM((16, 512), f32),
            pltpu.VMEM((16, 512), f32),
            pltpu.VMEM((128, 4096), bf16),
            pltpu.VMEM((1, 128), jnp.int32),
            pltpu.SMEM((1,), jnp.int32),
            pltpu.VMEM((NZ, 16, 512), bf16),
            pltpu.VMEM((2, NZ, 16, 256), bf16),
            pltpu.VMEM((2, NZ, 16, 256), bf16),
            pltpu.VMEM((2, NZ, 16, 256), bf16),
            pltpu.VMEM((4, 16, HD), bf16),
            pltpu.VMEM((4, 2, 2, 4, 2, 2, 16, HD), bf16),
            pltpu.VMEM((2, 8, 128, 512), bf16),
            pltpu.VMEM((4, 128, 512), bf16),
            pltpu.VMEM((128, 512), bf16),
            pltpu.VMEM((8, 128), jnp.int32),
            pltpu.VMEM((4, 8, 128), jnp.int32),
            pltpu.VMEM((128, 512), f32),
            pltpu.VMEM((32, 128, 512), bf16),
            pltpu.VMEM((32, 128, HD), f32),
            pltpu.VMEM((4, 8, 128, HD), bf16),
            pltpu.VMEM((4, 8, 128, HD), bf16),
            pltpu.VMEM((4, 4, 128, HD), bf16),
            dma((8,)),
            dma((12,)),
            dma((2, 2)),
            dma((2,)),
            dma((2,)),
            dma((8,)),
            dma((6,)),
            dma((4,)),
            dma((4, 3)),
            dma((4,)),
            dma((4, 2, 4)),
        ],
        compiler_params=pltpu.CompilerParams(
            collective_id=0, has_side_effects=True, vmem_limit_bytes=62 << 20
        ),
    )(
        grad_parts.reshape(NZ, 2, 16, 512),
        master_weight,
        moment_one,
        moment_two,
        queries[0],
        keys_in[0],
        hidden[0],
        segment_ids,
        packed_len,
    )
    new_master, new_first, new_second, _ = adam_update(
        grad_sum, master_weight, moment_one, moment_two
    )
    return (new_master, new_first, new_second, attended[None])


def solution(mesh):
    in_specs = (
        P("dp", "replica", None),
        P(("dp", "replica"), None),
        P(("dp", "replica"), None),
        P(("dp", "replica"), None),
        P("replica", "dp", None),
        P("replica", "dp", None),
        P("replica", "dp", None),
        P("replica", "dp"),
        P("replica"),
    )
    out_specs = (
        P(("dp", "replica"), None),
        P(("dp", "replica"), None),
        P(("dp", "replica"), None),
        P("replica", "dp", None),
    )
    return jax.shard_map(
        on_device, mesh=mesh, in_specs=in_specs, out_specs=out_specs, check_vma=False
    )
```
